256 devices in a mesh: tile: 64 (over y, x, z_lo, core), agent: 4 (over z_hi).
Axes of the slice: x: 4, y: 4, z: 8 (z_hi: 4, z_lo: 2; z = z_hi * 2 + z_lo), core: 2. Of those that a mesh axis runs over, the one named last changes fastest.
Arguments:
- agent_state: float32 [4, 1, 16, 1024, 256], P(None, None, None, 'tile', 'agent'), may hold values from 0 to 2
- measured: float32 [1, 16, 22528], P(None, None, ('tile', 'agent')), may hold values from 0 to 12
- bin_index: int32 [16, 1024, 256], P(None, 'tile', 'agent'), may hold values from 64 to 1342, as said below
- bin_frac: int32 [16, 1024, 256], P(None, 'tile', 'agent'), may hold values from 0 to 723, as said below
- patch_offsets: int32 [3], replicated, may hold values from 1 to 15
- agent_weights: float32 [4], replicated, may hold values from 0.5 to 2
- up_weight: bfloat16 [3, 256, 4096], P(None, None, 'agent'), may hold values from -0.375 to 0.375
- down_weight: bfloat16 [3, 4096, 256], P(None, 'agent'), may hold values from -0.09375 to 0.09375
Outputs:
- state_next: float32 [4, 1, 16, 1024, 256], P(None, None, None, 'tile', 'agent')
- data_fit: float32 [1, 16, 1024, 256], P(None, None, 'tile', 'agent')
The draws below stay inside these ranges and needn't reach their ends.
Inputs may be any that keep to these rules, and one draw needn't show every extreme that they name: bin_index[a, x, y] = floor(((x - 512) c_a + (y - 128) s_a) / 724) + 704 and bin_frac[a, x, y] is the remainder of that division, for whole numbers c_a, s_a of size at most 724 with c_a * c_a + s_a * s_a close to 524176, one pair an angle. bin_frac is the remainder that belongs to bin_index.
All inputs are finite; a program needn't handle non-finite values.
Results may differ from the reference program's by a relative error of at most 0.0003.
The reference program's roundings to bfloat16 on the way count: a program that leaves them out, or rounds other values in their place, can miss the bound.
Values may be sent and summed in bfloat16 or wider, within the bound.
No kernel may reach another device: no remote copies, remote signals or barrier semaphores. Data moves between devices by JAX's collectives and lax.ppermute only.
A program may use at most 64 MiB of HBM per device.

```python
import math
import jax
import jax.numpy as jnp
import numpy as np
from jax import lax

PATCH = 16
SLICES = 16
HIDDEN_SIZE = 4096
ANGLES = 16
GRAD_STEPS = 1
AGENTS = 4
TIMES = 1
NX = 1024
NY = 256
BINS = 1408
SINO = 22528


def geometry(key):
    turns = jax.random.randint(jax.random.fold_in(key, 11), (ANGLES,), 0, 4096)
    phases = np.arange(4096) * (2.0 * math.pi / 4096.0)
    cosines = jnp.asarray(np.floor(724.0 * np.cos(phases) + 0.5).astype(np.int32))
    sines = jnp.asarray(np.floor(724.0 * np.sin(phases) + 0.5).astype(np.int32))
    across = jnp.arange(NX, dtype=jnp.int32) - NX // 2
    along = jnp.arange(NY, dtype=jnp.int32) - NY // 2
    reach = cosines[turns][:, None, None] * across[None, :, None] + sines[turns][:, None, None] * along[None, None, :]
    return (reach // 724 + BINS // 2, reach % 724)


def draw_bin_index(key, part):
    return geometry(key)[0]


def draw_bin_frac(key, part):
    return geometry(key)[1]


def level_of(rng, shape, split, smallest, top_value):
    gain, own = 1.0, jax.random.fold_in(rng, 6)
    for dim, parts in split:
        steps = jnp.exp(jax.random.uniform(jax.random.fold_in(own, dim), (parts,), jnp.float32, smallest / len(split), top_value / len(split)))
        gain = gain * jnp.repeat(steps, shape[dim] // parts).reshape([-1 if axis == dim else 1 for axis in range(len(shape))])
    return gain


def normal_values(rng, shape, scale, most, split=(), kind=jnp.bfloat16):
    level = level_of(rng, shape, split, -0.22, 0.18) if split else 1.0
    entries = jax.random.normal(rng, shape, jnp.float32) * scale * level
    return jnp.minimum(jnp.maximum(entries, -most), most).astype(kind)


def setup_inputs(seed: int = 0) -> dict:
    key_of = jax.random.split(jax.random.key(seed), 9)
    agent_state = jnp.clip(2.0 * jax.random.uniform(key_of[0], (AGENTS, TIMES, SLICES, NX, NY), jnp.float32) ** level_of(key_of[0], (AGENTS, TIMES, SLICES, NX, NY), ((3, 64), (4, 4)), -0.2, 0.2), 0.0, 2.0)
    measured = jnp.clip(12.0 * jax.random.uniform(key_of[1], (TIMES, SLICES, SINO), jnp.float32) ** level_of(key_of[1], (TIMES, SLICES, SINO), ((2, 256),), -0.2, 0.2), 0.0, 12.0)
    bin_index = draw_bin_index(jax.random.fold_in(key_of[8], 71), 0)
    bin_frac = draw_bin_frac(jax.random.fold_in(key_of[8], 71), 0)
    patch_offsets = jax.random.randint(key_of[4], (AGENTS - 1,), 1, 16).astype(jnp.int32)
    agent_weights = jnp.clip(jnp.exp(jax.random.uniform(key_of[5], (AGENTS,), jnp.float32, math.log(0.5), math.log(2.0))), 0.5, 2.0)
    up_weight = normal_values(key_of[6], (AGENTS - 1, PATCH * PATCH, HIDDEN_SIZE), (PATCH * PATCH) ** -0.5, 0.375, ((2, 4),))
    down_weight = normal_values(key_of[7], (AGENTS - 1, HIDDEN_SIZE, PATCH * PATCH), HIDDEN_SIZE ** -0.5, 0.09375, ((1, 4),))
    return {"agent_state": agent_state, "measured": measured, "bin_index": bin_index, "bin_frac": bin_frac, "patch_offsets": patch_offsets, "agent_weights": agent_weights, "up_weight": up_weight, "down_weight": down_weight}


def network(patches, up_rows, down_rows):
    count = patches.shape[0]
    block = math.gcd(count, 4096)

    def apply_block(rows_in):
        hidden = jax.nn.relu(jnp.dot(rows_in, up_rows, preferred_element_type=jnp.float32)).astype(jnp.bfloat16)
        return jnp.dot(hidden, down_rows, preferred_element_type=jnp.float32)
    return lax.map(apply_block, patches.reshape(count // block, block, -1)).reshape(count, -1)

def data_agent(volume, measured, bin_index, bin_frac, factor):
    planes = volume.shape[0] * volume.shape[1]
    current = volume.reshape(planes, -1)
    lows = bin_index.reshape(ANGLES, -1)
    weights = bin_frac.reshape(ANGLES, -1).astype(jnp.float32) / 724.0
    target = measured.reshape(planes, ANGLES, BINS)
    for iteration in range(GRAD_STEPS):

        def project(carry, item):
            low_bin, weight = item
            row_sum = jnp.zeros((planes, BINS), jnp.float32)
            row_sum = row_sum.at[:, low_bin].add(current * weight[None, :])
            row_sum = row_sum.at[:, low_bin + 1].add(current * (1.0 - weight)[None, :])
            return (carry, row_sum)
        unused, sums = lax.scan(project, jnp.zeros((), jnp.float32), (lows, weights))
        misfit = factor * jnp.transpose(sums, (1, 0, 2)) - target

        def spread(total, item):
            low_bin, weight, resid = item
            total = total + jnp.take(resid, low_bin, axis=1) * weight[None, :]
            total = total + jnp.take(resid, low_bin + 1, axis=1) * (1.0 - weight)[None, :]
            return (total, None)
        back_sum, unused = lax.scan(spread, jnp.zeros_like(current), (lows, weights, jnp.transpose(misfit, (1, 0, 2))))
        current = current - factor * back_sum
    return current.reshape(volume.shape)

def in_plane(volume, shift, up_rows, down_rows):
    n_time, n_slice, n_row, n_col = volume.shape
    rolled = jnp.roll(volume, (-shift, -shift), axis=(2, 3))
    patches = rolled.reshape(n_time, n_slice, n_row // PATCH, PATCH, n_col // PATCH, PATCH)
    patches = patches.transpose(0, 1, 2, 4, 3, 5).reshape(-1, PATCH * PATCH)
    result = network(patches, up_rows, down_rows)
    result = result.reshape(n_time, n_slice, n_row // PATCH, n_col // PATCH, PATCH, PATCH)
    result = result.transpose(0, 1, 2, 4, 3, 5).reshape(n_time, n_slice, n_row, n_col)
    return jnp.roll(result, (shift, shift), axis=(2, 3))

def along_rows(volume, shift, up_rows, down_rows):
    n_time, n_slice, n_row, n_col = volume.shape
    rolled = jnp.roll(volume, -shift, axis=2)
    patches = rolled.reshape(n_time, n_slice, n_row // PATCH, PATCH, n_col)
    patches = patches.transpose(0, 2, 4, 1, 3).reshape(-1, n_slice * PATCH)
    result = network(patches, up_rows, down_rows)
    result = result.reshape(n_time, n_row // PATCH, n_col, n_slice, PATCH)
    result = result.transpose(0, 3, 1, 4, 2).reshape(n_time, n_slice, n_row, n_col)
    return jnp.roll(result, shift, axis=2)

def along_cols(volume, shift, up_rows, down_rows):
    n_time, n_slice, n_row, n_col = volume.shape
    rolled = jnp.roll(volume, -shift, axis=3)
    patches = rolled.reshape(n_time, n_slice, n_row, n_col // PATCH, PATCH)
    patches = patches.transpose(0, 2, 3, 1, 4).reshape(-1, n_slice * PATCH)
    result = network(patches, up_rows, down_rows)
    result = result.reshape(n_time, n_row, n_col // PATCH, n_slice, PATCH)
    result = result.transpose(0, 3, 1, 2, 4).reshape(n_time, n_slice, n_row, n_col)
    return jnp.roll(result, shift, axis=3)

def reference(agent_state, measured, bin_index, bin_frac, patch_offsets, agent_weights, up_weight, down_weight):
    factor = 1.0 / math.sqrt(ANGLES * (NX + NY))
    data_fit = data_agent(agent_state[0], measured, bin_index, bin_frac, factor)
    noisy = agent_state[1:].astype(jnp.bfloat16)
    first = agent_state[1] - in_plane(noisy[0], patch_offsets[0], up_weight[0], down_weight[0])
    second = agent_state[2] - along_rows(noisy[1], patch_offsets[1], up_weight[1], down_weight[1])
    third = agent_state[3] - along_cols(noisy[2], patch_offsets[2], up_weight[2], down_weight[2])
    answers = jnp.stack([data_fit, first, second, third])
    joining = agent_weights / jnp.sum(agent_weights)
    joined = lax.optimization_barrier(jnp.sum(joining[:, None, None, None, None] * (2.0 * answers - agent_state), axis=0))
    state_next = agent_state + joined[None] - answers
    return (state_next, data_fit)
```

```python
import functools
import math

import jax
import jax.numpy as jnp
from jax import lax
from jax.experimental import pallas as pl
from jax.experimental.pallas import tpu as pltpu
from jax.sharding import PartitionSpec as P

PATCH = 16
SCALE = 724
WINDOW = 128
ALIGN = 32


def extended_2(block, sides, width):
    for axis, dim in sides:
        count = lax.axis_size(axis)
        forward = [(i, i + 1) for i in range(count - 1)]
        forward.append((count - 1, 0))
        backward = [(target, source) for source, target in forward]
        low = lax.ppermute(
            lax.slice_in_dim(block, block.shape[dim] - width, None, axis=dim), axis, forward
        )
        high = lax.ppermute(lax.slice_in_dim(block, 0, width, axis=dim), axis, backward)
        block = jnp.concatenate([low, block, high], axis=dim)
    return block


def split_two(value):
    high = value.astype(jnp.bfloat16)
    return high, (value - high.astype(jnp.float32)).astype(jnp.bfloat16)


def window_starts(low):
    return (jnp.min(low, axis=1, keepdims=True) // ALIGN) * ALIGN


def one_hot(rel_row):
    spots = lax.broadcasted_iota(jnp.int32, (WINDOW, rel_row.shape[1]), 0)
    return jnp.where(spots == rel_row, 1.0, 0.0).astype(jnp.bfloat16)


def project_kernel(group_ref, u_ref, low_ref, frac_ref, meas_ref, out_ref, rel_ref, w_ref, start_ref):
    angles, planes, width = out_ref.shape
    low = low_ref[...]
    start = window_starts(low)
    rel_ref[...] = low - start
    w_ref[...] = frac_ref[...].astype(jnp.float32) * (1.0 / SCALE)
    start_ref[...] = jnp.broadcast_to(start.astype(jnp.float32), (angles, WINDOW))
    out_ref[...] = jnp.zeros_like(out_ref)
    owned = meas_ref.shape[1]
    out_ref[group_ref[0], :, WINDOW : WINDOW + owned] = meas_ref[...]
    lane = lax.broadcasted_iota(jnp.int32, (planes, WINDOW), 1)

    def body(a, carry):
        band = one_hot(rel_ref[pl.ds(a, 1), :])
        u = u_ref[...]
        near = u * w_ref[pl.ds(a, 1), :]
        near_hi, near_lo = split_two(near)
        far_hi, far_lo = split_two(u - near)
        terms = jnp.concatenate([near_hi, near_lo, far_hi, far_lo], axis=0)
        sums = lax.dot_general(
            terms, band, (((1,), (1,)), ((), ())), preferred_element_type=jnp.float32
        )
        at_low = sums[:planes] + sums[planes : 2 * planes]
        above = sums[2 * planes : 3 * planes] + sums[3 * planes :]
        piece = at_low + pltpu.roll(above, 1, 1)
        out_ref[a, :, :WINDOW] = jnp.where(lane == WINDOW - 1, start_ref[pl.ds(a, 1), :], piece)
        return carry

    lax.fori_loop(0, angles, body, 0, unroll=2)


def combine_kernel(factor, owned, got_ref, out_ref):
    count = got_ref.shape[0]
    step = WINDOW // ALIGN
    rows = 16
    got = got_ref[...]
    lane_all = lax.broadcasted_iota(jnp.int32, (count, WINDOW), 1)
    piece = jnp.where(lane_all < WINDOW - 1, got[:, :WINDOW], 0.0)
    block = got[:, WINDOW - 1 : WINDOW].astype(jnp.int32) // ALIGN
    slot = (block % step) * rows + block // step
    slots = lax.broadcasted_iota(jnp.int32, (count, step * rows), 1)
    route = jnp.where(slots == slot, 1.0, 0.0).astype(jnp.bfloat16)
    sums = lax.dot_general(
        route,
        jnp.concatenate(split_two(piece), axis=1),
        (((0,), (0,)), ((), ())),
        preferred_element_type=jnp.float32,
    )
    sums = sums[:, :WINDOW] + sums[:, WINDOW:]
    lane = lax.broadcasted_iota(jnp.int32, (rows, WINDOW), 1)
    row = lax.broadcasted_iota(jnp.int32, (rows, WINDOW), 0)
    sino = sums[:rows]
    for m in range(1, step):
        turned = pltpu.roll(sums[m * rows : (m + 1) * rows], m * ALIGN, 1)
        here = lane >= m * ALIGN
        sino = sino + jnp.where(here, turned, 0.0)
        sino = sino + pltpu.roll(jnp.where(here, 0.0, turned), 1, 0)
    taken = jnp.sum(got[:, WINDOW:].reshape(count // 16, 16, WINDOW), axis=0)
    taken = jnp.where(lax.broadcasted_iota(jnp.int32, taken.shape, 1) < owned, taken, 0.0)
    target = jnp.zeros_like(sino)
    for i in range(16):
        first, off = divmod(i * owned, WINDOW)
        turned = taken[i : i + 1]
        if off:
            turned = pltpu.roll(turned, off, 1)
        hit = ((row == first) & (lane >= off)) | ((row == first + 1) & (lane < off))
        target = target + jnp.where(hit, turned, 0.0)
    misfit = factor * sino - target
    views = [misfit]
    for m in range(1, step):
        turned = pltpu.roll(misfit, WINDOW - m * ALIGN, 1)
        views.append(
            jnp.where(lane < WINDOW - m * ALIGN, turned, pltpu.roll(turned, rows - 1, 0))
        )
    views = jnp.concatenate(views, axis=0)
    cut = jnp.dot(
        route, jnp.concatenate(split_two(views), axis=1), preferred_element_type=jnp.float32
    )
    out_ref[...] = cut[:, :WINDOW] + cut[:, WINDOW:]


def spread_kernel(factor, u_ref, low_ref, frac_ref, win_ref, out_ref, rel_ref, w_ref):
    angles, planes, width = win_ref.shape
    low = low_ref[...]
    rel_ref[...] = low - window_starts(low)
    w_ref[...] = frac_ref[...].astype(jnp.float32) * (1.0 / SCALE)

    def body(a, total):
        band = one_hot(rel_ref[pl.ds(a, 1), :])
        at_low = win_ref[a]
        above = pltpu.roll(at_low, WINDOW - 1, 1)
        terms = jnp.concatenate(split_two(at_low) + split_two(above), axis=0)
        picked = jnp.dot(terms, band, preferred_element_type=jnp.float32)
        near = picked[:planes] + picked[planes : 2 * planes]
        far = picked[2 * planes : 3 * planes] + picked[3 * planes :]
        w = w_ref[pl.ds(a, 1), :]
        return total + (far + w * (near - far))

    total = lax.fori_loop(0, angles, body, jnp.zeros(u_ref.shape, jnp.float32), unroll=2)
    out_ref[...] = u_ref[...] - factor * total


def data_agent(volume, bin_index, bin_frac, measured, factor, sino_width):
    angles = bin_index.shape[0]
    planes = volume.shape[0] * volume.shape[1]
    current = volume.reshape(planes, -1)
    pixels = current.shape[1]
    low = bin_index.reshape(angles, -1)
    frac = bin_frac.reshape(angles, -1)
    owned = measured.shape[2]
    group = (lax.axis_index("tile") * lax.axis_size("agent") // planes).astype(jnp.int32)
    vmem = pl.BlockSpec(memory_space=pltpu.VMEM)
    pieces = pl.pallas_call(
        project_kernel,
        out_shape=jax.ShapeDtypeStruct((angles, planes, 2 * WINDOW), jnp.float32),
        in_specs=[pl.BlockSpec(memory_space=pltpu.SMEM)] + [vmem] * 4,
        out_specs=vmem,
        scratch_shapes=[
            pltpu.VMEM((angles, pixels), jnp.int32),
            pltpu.VMEM((angles, pixels), jnp.float32),
            pltpu.VMEM((angles, WINDOW), jnp.float32),
        ],
        name="project",
    )(group.reshape(1), current, low, frac, measured.reshape(planes, owned))
    both = ("tile", "agent")
    got = lax.all_to_all(
        pieces.reshape(angles * planes, 2 * WINDOW), both, 0, 0, tiled=True
    )
    cut = pl.pallas_call(
        functools.partial(combine_kernel, factor, owned),
        out_shape=jax.ShapeDtypeStruct((angles * planes, WINDOW), jnp.float32),
        in_specs=[vmem],
        out_specs=vmem,
        name="combine",
    )(got)
    back = lax.all_to_all(cut, both, 0, 0, tiled=True)
    fit = pl.pallas_call(
        functools.partial(spread_kernel, factor),
        out_shape=jax.ShapeDtypeStruct((planes, pixels), jnp.float32),
        in_specs=[vmem] * 4,
        out_specs=vmem,
        scratch_shapes=[
            pltpu.VMEM((angles, pixels), jnp.int32),
            pltpu.VMEM((angles, pixels), jnp.float32),
        ],
        name="spread",
    )(current, low, frac, back.reshape(angles, planes, WINDOW))
    return fit.reshape(volume.shape)


def in_plane(extended, shift, apply_net):
    n_time, n_slice, ext_rows, ext_cols = extended.shape
    row_count = ext_rows - 2 * PATCH
    col_count = ext_cols - 2 * PATCH
    row_blocks = row_count // PATCH + 1
    col_blocks = col_count // PATCH + 1
    region = lax.dynamic_slice(
        extended, (0, 0, shift, shift), (n_time, n_slice, row_count + PATCH, col_count + PATCH)
    )
    patches = region.reshape(n_time, n_slice, row_blocks, PATCH, col_blocks, PATCH)
    patches = patches.transpose(0, 1, 2, 4, 3, 5).reshape(-1, PATCH * PATCH)
    result = apply_net(patches)
    result = result.reshape(n_time, n_slice, row_blocks, col_blocks, PATCH, PATCH)
    result = result.transpose(0, 1, 2, 4, 3, 5).reshape(
        n_time, n_slice, row_count + PATCH, col_count + PATCH
    )
    return lax.dynamic_slice(
        result, (0, 0, PATCH - shift, PATCH - shift), (n_time, n_slice, row_count, col_count)
    )


def along_rows(extended, shift, apply_net):
    n_time, n_slice, ext_rows, ext_cols = extended.shape
    row_count = ext_rows - 2 * PATCH
    col_count = ext_cols - 2 * PATCH
    row_blocks = row_count // PATCH + 1
    region = lax.dynamic_slice(
        extended, (0, 0, shift, PATCH), (n_time, n_slice, row_count + PATCH, col_count)
    )
    patches = region.reshape(n_time, n_slice, row_blocks, PATCH, col_count)
    patches = patches.transpose(0, 2, 4, 1, 3).reshape(-1, n_slice * PATCH)
    result = apply_net(patches)
    result = result.reshape(n_time, row_blocks, col_count, n_slice, PATCH)
    result = result.transpose(0, 3, 1, 4, 2).reshape(n_time, n_slice, row_count + PATCH, col_count)
    return lax.dynamic_slice(
        result, (0, 0, PATCH - shift, 0), (n_time, n_slice, row_count, col_count)
    )


def along_cols(extended, shift, apply_net):
    n_time, n_slice, ext_rows, ext_cols = extended.shape
    row_count = ext_rows - 2 * PATCH
    col_count = ext_cols - 2 * PATCH
    col_blocks = col_count // PATCH + 1
    region = lax.dynamic_slice(
        extended, (0, 0, PATCH, shift), (n_time, n_slice, row_count, col_count + PATCH)
    )
    patches = region.reshape(n_time, n_slice, row_count, col_blocks, PATCH)
    patches = patches.transpose(0, 2, 3, 1, 4).reshape(-1, n_slice * PATCH)
    result = apply_net(patches)
    result = result.reshape(n_time, row_count, col_blocks, n_slice, PATCH)
    result = result.transpose(0, 3, 1, 2, 4).reshape(n_time, n_slice, row_count, col_count + PATCH)
    return lax.dynamic_slice(
        result, (0, 0, 0, PATCH - shift), (n_time, n_slice, row_count, col_count)
    )


def shards(
    agent_state, measured, bin_index, bin_frac, patch_offsets, agent_weights, up_weight, down_weight
):
    row_count = agent_state.shape[3]
    col_count = agent_state.shape[4]
    tile_count = lax.axis_size("tile")
    agent_count = lax.axis_size("agent")
    full_rows = row_count * tile_count
    full_cols = col_count * agent_count
    angles = bin_index.shape[0]
    factor = 1.0 / math.sqrt(angles * (full_rows + full_cols))
    sino_width = measured.shape[2] * tile_count * agent_count
    data_fit = data_agent(agent_state[0], bin_index, bin_frac, measured, factor, sino_width)
    noisy = agent_state[1:].astype(jnp.bfloat16)
    extended = extended_2(noisy, (("tile", 3), ("agent", 4)), PATCH)

    def denoiser(which):

        def apply_net(patches):
            hidden = jax.nn.relu(
                jnp.dot(
                    lax.all_gather(patches, "agent", axis=0, tiled=True),
                    up_weight[which],
                    preferred_element_type=jnp.float32,
                )
            ).astype(jnp.bfloat16)
            terms = jnp.dot(hidden, down_weight[which], preferred_element_type=jnp.float32)
            return lax.psum_scatter(terms, "agent", scatter_dimension=0, tiled=True)

        return apply_net

    first = agent_state[1] - in_plane(extended[0], patch_offsets[0], denoiser(0))
    second = agent_state[2] - along_rows(extended[1], patch_offsets[1], denoiser(1))
    third = agent_state[3] - along_cols(extended[2], patch_offsets[2], denoiser(2))
    answers = jnp.stack([data_fit, first, second, third])
    joining = agent_weights / jnp.sum(agent_weights)
    joined = jnp.sum(joining[:, None, None, None, None] * (2.0 * answers - agent_state), axis=0)
    state_next = agent_state + joined[None] - answers
    return (state_next, data_fit)


def solution(mesh):
    placed = (
        P(None, None, None, "tile", "agent"),
        P(None, None, ("tile", "agent")),
        P(None, "tile", "agent"),
        P(None, "tile", "agent"),
        P(),
        P(),
        P(None, None, "agent"),
        P(None, "agent", None),
    )
    return jax.shard_map(
        shards,
        mesh=mesh,
        in_specs=placed,
        out_specs=(P(None, None, None, "tile", "agent"), P(None, None, "tile", "agent")),
        check_vma=False,
    )
```

```python
import functools
import math

import jax
import jax.numpy as jnp
from jax import lax
from jax.experimental import pallas as pl
from jax.experimental.pallas import tpu as pltpu
from jax.sharding import PartitionSpec as P

PATCH = 16
SCALE = 724
WINDOW = 128
ALIGN = 32


def split_two(value):
    high = value.astype(jnp.bfloat16)
    return high, (value - high.astype(jnp.float32)).astype(jnp.bfloat16)


def window_starts(low):
    return (jnp.min(low, axis=1, keepdims=True) // ALIGN) * ALIGN


def one_hot(rel_row):
    spots = lax.broadcasted_iota(jnp.int32, (WINDOW, rel_row.shape[1]), 0)
    return jnp.where(spots == rel_row, 1.0, 0.0).astype(jnp.bfloat16)


def project_kernel(
    group_ref, state_ref, bin_ref, num_ref, meas_ref, out_ref, u_ref, rel_ref, w_ref, start_ref
):
    angles, planes, _ = out_ref.shape
    cols = bin_ref.shape[2]
    for x in range(bin_ref.shape[1]):
        span = slice(x * cols, (x + 1) * cols)
        u_ref[:, span] = state_ref[0, 0, :, x, :]
        rel_ref[:, span] = bin_ref[:, x, :]
        w_ref[:, span] = num_ref[:, x, :].astype(jnp.float32) * (1.0 / SCALE)
    low = rel_ref[...]
    start = window_starts(low)
    rel_ref[...] = low - start
    start_ref[...] = jnp.broadcast_to(start.astype(jnp.float32), (angles, WINDOW))
    out_ref[...] = jnp.zeros_like(out_ref)
    owned = meas_ref.shape[2]
    out_ref[group_ref[0], :, WINDOW : WINDOW + owned] = meas_ref[0]
    lane = lax.broadcasted_iota(jnp.int32, (planes, WINDOW), 1)

    def body(a, carry):
        band = one_hot(rel_ref[pl.ds(a, 1), :])
        u = u_ref[...]
        near = u * w_ref[pl.ds(a, 1), :]
        near_hi, near_lo = split_two(near)
        far_hi, far_lo = split_two(u - near)
        terms = jnp.concatenate([near_hi, near_lo, far_hi, far_lo], axis=0)
        sums = lax.dot_general(
            terms, band, (((1,), (1,)), ((), ())), preferred_element_type=jnp.float32
        )
        at_low = sums[:planes] + sums[planes : 2 * planes]
        above = sums[2 * planes : 3 * planes] + sums[3 * planes :]
        piece = at_low + pltpu.roll(above, 1, 1)
        out_ref[a, :, :WINDOW] = jnp.where(lane == WINDOW - 1, start_ref[pl.ds(a, 1), :], piece)
        return carry

    lax.fori_loop(0, angles, body, 0, unroll=2)


def combine_kernel(factor, owned, got_ref, out_ref):
    count = got_ref.shape[0]
    step = WINDOW // ALIGN
    rows = 16
    got = got_ref[...]
    lane_all = lax.broadcasted_iota(jnp.int32, (count, WINDOW), 1)
    piece = jnp.where(lane_all < WINDOW - 1, got[:, :WINDOW], 0.0)
    block = got[:, WINDOW - 1 : WINDOW].astype(jnp.int32) // ALIGN
    slot = (block % step) * rows + block // step
    slots = lax.broadcasted_iota(jnp.int32, (count, step * rows), 1)
    route = jnp.where(slots == slot, 1.0, 0.0).astype(jnp.bfloat16)
    sums = lax.dot_general(
        route,
        jnp.concatenate(split_two(piece), axis=1),
        (((0,), (0,)), ((), ())),
        preferred_element_type=jnp.float32,
    )
    sums = sums[:, :WINDOW] + sums[:, WINDOW:]
    lane = lax.broadcasted_iota(jnp.int32, (rows, WINDOW), 1)
    row = lax.broadcasted_iota(jnp.int32, (rows, WINDOW), 0)
    sino = sums[:rows]
    for m in range(1, step):
        turned = pltpu.roll(sums[m * rows : (m + 1) * rows], m * ALIGN, 1)
        here = lane >= m * ALIGN
        sino = sino + jnp.where(here, turned, 0.0)
        sino = sino + pltpu.roll(jnp.where(here, 0.0, turned), 1, 0)
    taken = jnp.sum(got[:, WINDOW:].reshape(count // 16, 16, WINDOW), axis=0)
    taken = jnp.where(lax.broadcasted_iota(jnp.int32, taken.shape, 1) < owned, taken, 0.0)
    target = jnp.zeros_like(sino)
    for i in range(16):
        first, off = divmod(i * owned, WINDOW)
        turned = taken[i : i + 1]
        if off:
            turned = pltpu.roll(turned, off, 1)
        hit = ((row == first) & (lane >= off)) | ((row == first + 1) & (lane < off))
        target = target + jnp.where(hit, turned, 0.0)
    misfit = factor * sino - target
    views = [misfit]
    for m in range(1, step):
        turned = pltpu.roll(misfit, WINDOW - m * ALIGN, 1)
        views.append(
            jnp.where(lane < WINDOW - m * ALIGN, turned, pltpu.roll(turned, rows - 1, 0))
        )
    views = jnp.concatenate(views, axis=0)
    cut = jnp.dot(
        route, jnp.concatenate(split_two(views), axis=1), preferred_element_type=jnp.float32
    )
    out_ref[...] = cut[:, :WINDOW] + cut[:, WINDOW:]


def shift_kernel(offset_ref, own_ref, next_ref, out_ref):
    rows = own_ref.shape[2]
    for k in range(2):
        o = offset_ref[k]
        own = pltpu.roll(own_ref[k].astype(jnp.float32), rows - o, 1)
        more = pltpu.roll(next_ref[k].astype(jnp.float32), rows - o, 1)
        row = lax.broadcasted_iota(jnp.int32, own.shape, 1)
        out_ref[k] = jnp.where(row < rows - o, own, more).astype(out_ref.dtype)
    out_ref[2] = own_ref[2]


def swap_slabs(slabs):
    lane = lax.broadcasted_iota(jnp.int32, slabs[0].shape, 1)
    width = slabs[0].shape[1]
    slabs = list(slabs)
    for step in (1, 2, 4, 8):
        odd = (lane & step) != 0
        for i in range(len(slabs)):
            if i & step:
                continue
            first, second = slabs[i], slabs[i + step]
            slabs[i] = jnp.where(odd, pltpu.roll(second, step, 1), first)
            slabs[i + step] = jnp.where(odd, second, pltpu.roll(first, width - step, 1))
    return slabs


def swap_rows(slab):
    width = slab.shape[1]
    top, low = slab[:8], slab[8:]
    lane = lax.broadcasted_iota(jnp.int32, top.shape, 1)
    row = lax.broadcasted_iota(jnp.int32, top.shape, 0)
    odd = (lane & 8) != 0
    top, low = (
        jnp.where(odd, pltpu.roll(low, 8, 1), top),
        jnp.where(odd, low, pltpu.roll(top, width - 8, 1)),
    )
    halves = []
    for half in (top, low):
        for step in (1, 2, 4):
            odd_lane, odd_row = (lane & step) != 0, (row & step) != 0
            up = pltpu.roll(pltpu.roll(half, 8 - step, 0), step, 1)
            down = pltpu.roll(pltpu.roll(half, step, 0), width - step, 1)
            other = jnp.where(odd_lane, up, down)
            half = jnp.where(odd_lane == odd_row, half, other)
        halves.append(half)
    return jnp.concatenate(halves, axis=0)


def denoise_kernel(offset_ref, p0, p1, p2, p3, up_ref, down_ref, o0, o1, o2, o3):
    side = PATCH
    size = side * side
    row = lax.broadcasted_iota(jnp.int32, (size, size), 0)
    col = lax.broadcasted_iota(jnp.int32, (size, size), 1)
    turned = (row % side) * side + row // side
    exchange = jnp.where(col == turned, 1.0, 0.0).astype(jnp.bfloat16)
    lane = lax.broadcasted_iota(jnp.int32, (size // 2, WINDOW), 1)
    left = lane < WINDOW // 2
    wide = lax.broadcasted_iota(jnp.int32, (size, WINDOW), 1)

    def joined(a, b):
        a = a.reshape(size // 2, WINDOW).astype(jnp.float32)
        b = b.reshape(size // 2, WINDOW).astype(jnp.float32)
        early = jnp.where(left, a, pltpu.roll(b, WINDOW // 2, 1))
        late = jnp.where(left, pltpu.roll(a, WINDOW // 2, 1), b)
        return jnp.concatenate([early, late], axis=0)

    def slabs_of(half):
        return [half[i * side : (i + 1) * side] for i in range(side)]

    def arrange(which, half):
        if which == 0:
            return jnp.concatenate(swap_slabs(slabs_of(half)), axis=0)
        if which == 2:
            return jnp.concatenate([swap_rows(slab) for slab in slabs_of(half)], axis=0)
        return half

    for k in range(3):
        halves = [joined(p0[k], p1[k]), joined(p2[k], p3[k])]
        if k != 1:
            o = offset_ref[k]
            a, b = [pltpu.roll(half, WINDOW - o, 1) for half in halves]
            inside = wide < WINDOW - o
            halves = [jnp.where(inside, a, b), jnp.where(inside, b, a)]
        halves = [arrange(k, half) for half in halves]
        patches = jnp.concatenate([half.T for half in halves], axis=0).astype(jnp.bfloat16)
        down = down_ref[k]
        if k == 0:
            patches = jnp.dot(
                patches, exchange, preferred_element_type=jnp.float32
            ).astype(jnp.bfloat16)
            down = jnp.dot(down, exchange, preferred_element_type=jnp.float32).astype(jnp.bfloat16)
        hidden = jnp.dot(patches, up_ref[k], preferred_element_type=jnp.float32)
        hidden = jnp.maximum(hidden, 0.0).astype(jnp.bfloat16)
        result = jnp.dot(hidden, down, preferred_element_type=jnp.float32)
        halves = [arrange(k, result[:WINDOW].T), arrange(k, result[WINDOW:].T)]
        if k != 1:
            a, b = [pltpu.roll(half, o, 1) for half in halves]
            inside = wide >= o
            halves = [jnp.where(inside, a, b), jnp.where(inside, b, a)]
        for half, first, second in ((halves[0], o0, o1), (halves[1], o2, o3)):
            early, late = half[: size // 2], half[size // 2 :]
            first[k] = jnp.where(left, early, pltpu.roll(late, WINDOW // 2, 1)).reshape(
                first.shape[1:]
            )
            second[k] = jnp.where(left, pltpu.roll(early, WINDOW // 2, 1), late).reshape(
                second.shape[1:]
            )


def finish_kernel(
    factor, offset_ref, weight_ref, state_ref, u_ref, rel_ref, w_ref, win_ref, net_ref, prev_ref,
    next_ref, fit_ref,
):
    angles, planes, _ = win_ref.shape

    def body(a, total):
        band = one_hot(rel_ref[pl.ds(a, 1), :])
        at_low = win_ref[a]
        above = pltpu.roll(at_low, WINDOW - 1, 1)
        terms = jnp.concatenate(split_two(at_low) + split_two(above), axis=0)
        picked = jnp.dot(terms, band, preferred_element_type=jnp.float32)
        near = picked[:planes] + picked[planes : 2 * planes]
        far = picked[2 * planes : 3 * planes] + picked[3 * planes :]
        w = w_ref[pl.ds(a, 1), :]
        return total + (far + w * (near - far))

    total = lax.fori_loop(0, angles, body, jnp.zeros(u_ref.shape, jnp.float32), unroll=2)
    fit = u_ref[...] - factor * total
    rows, cols = fit_ref.shape[2:]
    for x in range(rows):
        fit_ref[0, :, x, :] = fit[:, x * cols : (x + 1) * cols]

    raw = [jnp.full((1, cols), weight_ref[i], jnp.float32) for i in range(4)]
    whole = raw[0] + raw[1] + raw[2] + raw[3]
    share = [value / whole for value in raw]
    row = lax.broadcasted_iota(jnp.int32, net_ref.shape[1:], 1)
    nets = []
    for k in range(3):
        net = net_ref[k]
        if k < 2:
            o = offset_ref[k]
            net = jnp.where(row >= o, pltpu.roll(net, o, 1), pltpu.roll(prev_ref[k], o, 1))
        nets.append((net[:, :, :cols], pltpu.roll(net, WINDOW - cols, 2)[:, :, :cols]))
    count = planes // 2
    for part in range(2):
        span = slice(part * count, (part + 1) * count)
        held = state_ref[0, 0, span]
        answer = fit_ref[0, span]
        joined = share[0] * (2.0 * answer - held)
        for k in range(3):
            joined = joined + share[k + 1] * (state_ref[k + 1, 0, span] - 2.0 * nets[k][part])
        next_ref[0, 0, span] = held + joined - answer
        for k in range(3):
            next_ref[k + 1, 0, span] = joined + nets[k][part]


VMEM = pl.BlockSpec(memory_space=pltpu.VMEM)
SMEM = pl.BlockSpec(memory_space=pltpu.SMEM)


def hop(value, axis, step):
    count = lax.axis_size(axis)
    return lax.ppermute(value, axis, [(i, (i + step) % count) for i in range(count)])


def shards(
    agent_state, measured, bin_index, bin_frac, patch_offsets, agent_weights, up_weight, down_weight
):
    planes, row_count, col_count = agent_state.shape[2:]
    tile_count = lax.axis_size("tile")
    agent_count = lax.axis_size("agent")
    angles = bin_index.shape[0]
    pixels = row_count * col_count
    factor = 1.0 / math.sqrt(angles * (row_count * tile_count + col_count * agent_count))
    both = ("tile", "agent")
    f32 = jnp.float32

    noisy = agent_state[1:, 0].astype(jnp.bfloat16)
    packed = jnp.concatenate([noisy[:, : planes // 2], noisy[:, planes // 2 :]], axis=-1)
    following = hop(packed[:2], "tile", -1)

    group = (lax.axis_index("tile") * agent_count // planes).astype(jnp.int32)
    pieces, flat, rel, near = pl.pallas_call(
        project_kernel,
        out_shape=[
            jax.ShapeDtypeStruct((angles, planes, 2 * WINDOW), f32),
            jax.ShapeDtypeStruct((planes, pixels), f32),
            jax.ShapeDtypeStruct((angles, pixels), jnp.int32),
            jax.ShapeDtypeStruct((angles, pixels), f32),
        ],
        in_specs=[SMEM] + [VMEM] * 4,
        out_specs=[VMEM] * 4,
        scratch_shapes=[pltpu.VMEM((angles, WINDOW), f32)],
        name="project",
    )(group.reshape(1), agent_state[:1], bin_index, bin_frac, measured)

    region = pl.pallas_call(
        shift_kernel,
        out_shape=jax.ShapeDtypeStruct(packed.shape, packed.dtype),
        in_specs=[SMEM, VMEM, VMEM],
        out_specs=VMEM,
        name="shift",
    )(patch_offsets, packed, following)
    others = [hop(region, "agent", -step) for step in range(1, agent_count)]

    got = lax.all_to_all(pieces.reshape(angles * planes, 2 * WINDOW), both, 0, 0, tiled=True)
    cut = pl.pallas_call(
        functools.partial(combine_kernel, factor, measured.shape[2]),
        out_shape=jax.ShapeDtypeStruct((angles * planes, WINDOW), f32),
        in_specs=[VMEM],
        out_specs=VMEM,
        name="combine",
    )(got)

    parts = pl.pallas_call(
        denoise_kernel,
        out_shape=[jax.ShapeDtypeStruct(packed.shape, f32)] * 4,
        in_specs=[SMEM] + [VMEM] * 6,
        out_specs=[VMEM] * 4,
        name="denoise",
    )(patch_offsets, region, *others, up_weight, down_weight)
    arrived = [hop(parts[step], "agent", step) for step in range(1, agent_count)]

    back = lax.all_to_all(cut, both, 0, 0, tiled=True)
    nets = parts[0] + arrived[0] + arrived[1] + arrived[2]
    previous = hop(nets[:2], "tile", 1)

    return pl.pallas_call(
        functools.partial(finish_kernel, factor),
        out_shape=[
            jax.ShapeDtypeStruct(agent_state.shape, f32),
            jax.ShapeDtypeStruct(agent_state.shape[1:], f32),
        ],
        in_specs=[SMEM, SMEM] + [VMEM] * 7,
        out_specs=[VMEM, VMEM],
        name="finish",
    )(
        patch_offsets, agent_weights, agent_state, flat, rel, near,
        back.reshape(angles, planes, WINDOW), nets, previous,
    )


def solution(mesh):
    placed = (
        P(None, None, None, "tile", "agent"),
        P(None, None, ("tile", "agent")),
        P(None, "tile", "agent"),
        P(None, "tile", "agent"),
        P(),
        P(),
        P(None, None, "agent"),
        P(None, "agent", None),
    )
    return jax.shard_map(
        shards,
        mesh=mesh,
        in_specs=placed,
        out_specs=(P(None, None, None, "tile", "agent"), P(None, None, "tile", "agent")),
        check_vma=False,
    )
```

```python
import functools
import math

import jax
import jax.numpy as jnp
from jax import lax
from jax.experimental import pallas as pl
from jax.experimental.pallas import tpu as pltpu
from jax.sharding import PartitionSpec as P


PATCH = 16
SCALE = 724
WINDOW = 128
ALIGN = 32


def split_two(value):
    high = value.astype(jnp.bfloat16)
    return high, (value - high.astype(jnp.float32)).astype(jnp.bfloat16)


def window_starts(low):
    return (jnp.min(low, axis=1, keepdims=True) // ALIGN) * ALIGN


def one_hot(rel_row):
    spots = lax.broadcasted_iota(jnp.int32, (WINDOW, rel_row.shape[1]), 0)
    return jnp.where(spots == rel_row, 1.0, 0.0).astype(jnp.bfloat16)


def project_kernel(
    group_ref, state_ref, bin_ref, num_ref, meas_ref, out_ref, u_ref, rel_ref, w_ref, start_ref
):
    angles, rows, cols = bin_ref.shape
    planes = state_ref.shape[2]
    for x in range(rows):
        span = slice(x * cols, (x + 1) * cols)
        u_ref[:, span] = state_ref[0, 0, :, x, :]
        rel_ref[:, span] = bin_ref[:, x, :]
        w_ref[:, span] = num_ref[:, x, :].astype(jnp.float32) * (1.0 / SCALE)
    low = rel_ref[...]
    start = window_starts(low)
    rel_ref[...] = low - start
    start_ref[...] = jnp.broadcast_to(start.astype(jnp.float32), (angles, WINDOW))
    out_ref[...] = jnp.zeros_like(out_ref)
    owned = meas_ref.shape[2]
    mine = pl.multiple_of(group_ref[0] * (2 * planes), 2 * planes)
    out_ref[pl.ds(mine + 1, planes, stride=2), :owned] = meas_ref[0]
    lane = lax.broadcasted_iota(jnp.int32, (planes, WINDOW), 1)

    def body(a, carry):
        band = one_hot(rel_ref[pl.ds(a, 1), :])
        u = u_ref[...]
        near = u * w_ref[pl.ds(a, 1), :]
        near_hi, near_lo = split_two(near)
        far_hi, far_lo = split_two(u - near)
        terms = jnp.concatenate([near_hi, near_lo, far_hi, far_lo], axis=0)
        sums = lax.dot_general(
            terms, band, (((1,), (1,)), ((), ())), preferred_element_type=jnp.float32
        )
        at_low = sums[:planes] + sums[planes : 2 * planes]
        above = sums[2 * planes : 3 * planes] + sums[3 * planes :]
        piece = at_low + pltpu.roll(above, 1, 1)
        piece = jnp.where(lane == WINDOW - 1, start_ref[pl.ds(a, 1), :], piece)
        first = pl.multiple_of(a * (2 * planes), 2 * planes)
        out_ref[pl.ds(first, planes, stride=2), :] = piece
        return carry

    lax.fori_loop(0, angles, body, 0, unroll=2)


def combine_kernel(factor, owned, got_ref, out_ref):
    count = got_ref.shape[0] // 2
    step = WINDOW // ALIGN
    rows = 16
    got = got_ref[pl.ds(0, count, stride=2), :]
    lane_all = lax.broadcasted_iota(jnp.int32, (count, WINDOW), 1)
    piece = jnp.where(lane_all < WINDOW - 1, got, 0.0)
    block = got[:, WINDOW - 1 :].astype(jnp.int32) // ALIGN
    slot = (block % step) * rows + block // step
    slots = lax.broadcasted_iota(jnp.int32, (count, step * rows), 1)
    route = jnp.where(slots == slot, 1.0, 0.0).astype(jnp.bfloat16)
    sums = lax.dot_general(
        route,
        jnp.concatenate(split_two(piece), axis=1),
        (((0,), (0,)), ((), ())),
        preferred_element_type=jnp.float32,
    )
    sums = sums[:, :WINDOW] + sums[:, WINDOW:]
    lane = lax.broadcasted_iota(jnp.int32, (rows, WINDOW), 1)
    row = lax.broadcasted_iota(jnp.int32, (rows, WINDOW), 0)
    sino = sums[:rows]
    for m in range(1, step):
        turned = pltpu.roll(sums[m * rows : (m + 1) * rows], m * ALIGN, 1)
        here = lane >= m * ALIGN
        sino = sino + jnp.where(here, turned, 0.0)
        sino = sino + pltpu.roll(jnp.where(here, 0.0, turned), 1, 0)
    sent = got_ref[pl.ds(1, count, stride=2), :]
    taken = jnp.sum(sent.reshape(count // 16, 16, WINDOW), axis=0)
    taken = jnp.where(lax.broadcasted_iota(jnp.int32, taken.shape, 1) < owned, taken, 0.0)
    target = jnp.zeros_like(sino)
    for i in range(16):
        first, off = divmod(i * owned, WINDOW)
        turned = taken[i : i + 1]
        if off:
            turned = pltpu.roll(turned, off, 1)
        hit = ((row == first) & (lane >= off)) | ((row == first + 1) & (lane < off))
        target = target + jnp.where(hit, turned, 0.0)
    misfit = factor * sino - target
    views = [misfit]
    for m in range(1, step):
        turned = pltpu.roll(misfit, WINDOW - m * ALIGN, 1)
        views.append(
            jnp.where(lane < WINDOW - m * ALIGN, turned, pltpu.roll(turned, rows - 1, 0))
        )
    views = jnp.concatenate(views, axis=0)
    cut = jnp.dot(
        route, jnp.concatenate(split_two(views), axis=1), preferred_element_type=jnp.float32
    )
    out_ref[...] = cut[:, :WINDOW] + cut[:, WINDOW:]


def pack_kernel(state_ref, head_ref, tail_ref):
    half = state_ref.shape[2] // 2
    cols = state_ref.shape[4]
    for k in range(3):
        out = head_ref.at[k] if k < 2 else tail_ref.at[0]
        out[:, :, :cols] = state_ref[k + 1, 0, :half].astype(out.dtype)
        out[:, :, cols:] = state_ref[k + 1, 0, half:].astype(out.dtype)


def shift_kernel(offset_ref, head_ref, tail_ref, next_ref, out_ref):
    rows = head_ref.shape[2]
    for k in range(2):
        o = offset_ref[k]
        own = pltpu.roll(head_ref[k].astype(jnp.float32), rows - o, 1)
        more = pltpu.roll(next_ref[k].astype(jnp.float32), rows - o, 1)
        row = lax.broadcasted_iota(jnp.int32, own.shape, 1)
        out_ref[k] = jnp.where(row < rows - o, own, more).astype(out_ref.dtype)
    out_ref[2] = tail_ref[0]


def swap_slabs(slabs):
    lane = lax.broadcasted_iota(jnp.int32, slabs[0].shape, 1)
    width = slabs[0].shape[1]
    slabs = list(slabs)
    for step in (1, 2, 4, 8):
        odd = (lane & step) != 0
        for i in range(len(slabs)):
            if i & step:
                continue
            first, second = slabs[i], slabs[i + step]
            slabs[i] = jnp.where(odd, pltpu.roll(second, step, 1), first)
            slabs[i + step] = jnp.where(odd, second, pltpu.roll(first, width - step, 1))
    return slabs


def swap_rows(slab):
    width = slab.shape[1]
    top, low = slab[:8], slab[8:]
    lane = lax.broadcasted_iota(jnp.int32, top.shape, 1)
    row = lax.broadcasted_iota(jnp.int32, top.shape, 0)
    odd = (lane & 8) != 0
    top, low = (
        jnp.where(odd, pltpu.roll(low, 8, 1), top),
        jnp.where(odd, low, pltpu.roll(top, width - 8, 1)),
    )
    halves = []
    for half in (top, low):
        for step in (1, 2, 4):
            odd_lane, odd_row = (lane & step) != 0, (row & step) != 0
            up = pltpu.roll(pltpu.roll(half, 8 - step, 0), step, 1)
            down = pltpu.roll(pltpu.roll(half, step, 0), width - step, 1)
            other = jnp.where(odd_lane, up, down)
            half = jnp.where(odd_lane == odd_row, half, other)
        halves.append(half)
    return jnp.concatenate(halves, axis=0)


def denoise_kernel(offset_ref, p0, p1, p2, p3, up_ref, down_ref, o0, o1, o2, o3):
    side = PATCH
    size = side * side
    row = lax.broadcasted_iota(jnp.int32, (size, size), 0)
    col = lax.broadcasted_iota(jnp.int32, (size, size), 1)
    turned = (row % side) * side + row // side
    exchange = jnp.where(col == turned, 1.0, 0.0).astype(jnp.bfloat16)
    lane = lax.broadcasted_iota(jnp.int32, (size // 2, WINDOW), 1)
    left = lane < WINDOW // 2
    wide = lax.broadcasted_iota(jnp.int32, (size, WINDOW), 1)

    def joined(a, b):
        a = a.reshape(size // 2, WINDOW).astype(jnp.float32)
        b = b.reshape(size // 2, WINDOW).astype(jnp.float32)
        early = jnp.where(left, a, pltpu.roll(b, WINDOW // 2, 1))
        late = jnp.where(left, pltpu.roll(a, WINDOW // 2, 1), b)
        return jnp.concatenate([early, late], axis=0)

    def slabs_of(half):
        return [half[i * side : (i + 1) * side] for i in range(side)]

    def arrange(which, half):
        if which == 0:
            return jnp.concatenate(swap_slabs(slabs_of(half)), axis=0)
        if which == 2:
            return jnp.concatenate([swap_rows(slab) for slab in slabs_of(half)], axis=0)
        return half

    for k in range(3):
        halves = [joined(p0[k], p1[k]), joined(p2[k], p3[k])]
        if k != 1:
            o = offset_ref[k]
            a, b = [pltpu.roll(half, WINDOW - o, 1) for half in halves]
            inside = wide < WINDOW - o
            halves = [jnp.where(inside, a, b), jnp.where(inside, b, a)]
        halves = [arrange(k, half) for half in halves]
        patches = jnp.concatenate([half.T for half in halves], axis=0).astype(jnp.bfloat16)
        down = down_ref[k]
        if k == 0:
            patches = jnp.dot(
                patches, exchange, preferred_element_type=jnp.float32
            ).astype(jnp.bfloat16)
            down = jnp.dot(down, exchange, preferred_element_type=jnp.float32).astype(jnp.bfloat16)
        hidden = jnp.dot(patches, up_ref[k], preferred_element_type=jnp.float32)
        hidden = jnp.maximum(hidden, 0.0).astype(jnp.bfloat16)
        result = jnp.dot(hidden, down, preferred_element_type=jnp.float32)
        halves = [arrange(k, result[:WINDOW].T), arrange(k, result[WINDOW:].T)]
        if k != 1:
            a, b = [pltpu.roll(half, o, 1) for half in halves]
            inside = wide >= o
            halves = [jnp.where(inside, a, b), jnp.where(inside, b, a)]
        for half, first, second in ((halves[0], o0, o1), (halves[1], o2, o3)):
            early, late = half[: size // 2], half[size // 2 :]
            first[k] = jnp.where(left, early, pltpu.roll(late, WINDOW // 2, 1)).reshape(
                first.shape[1:]
            )
            second[k] = jnp.where(left, pltpu.roll(early, WINDOW // 2, 1), late).reshape(
                second.shape[1:]
            )


def finish_kernel(
    factor, offset_ref, weight_ref, state_ref, u_ref, rel_ref, w_ref, win_ref, net_ref, prev_ref,
    next_ref, fit_ref,
):
    angles, planes, _ = win_ref.shape

    def body(a, total):
        band = one_hot(rel_ref[pl.ds(a, 1), :])
        at_low = win_ref[a]
        above = pltpu.roll(at_low, WINDOW - 1, 1)
        terms = jnp.concatenate(split_two(at_low) + split_two(above), axis=0)
        picked = jnp.dot(terms, band, preferred_element_type=jnp.float32)
        near = picked[:planes] + picked[planes : 2 * planes]
        far = picked[2 * planes : 3 * planes] + picked[3 * planes :]
        w = w_ref[pl.ds(a, 1), :]
        return total + (far + w * (near - far))

    total = lax.fori_loop(0, angles, body, jnp.zeros(u_ref.shape, jnp.float32), unroll=2)
    fit = u_ref[...] - factor * total
    rows, cols = fit_ref.shape[2:]
    for x in range(rows):
        fit_ref[0, :, x, :] = fit[:, x * cols : (x + 1) * cols]

    raw = [jnp.full((1, cols), weight_ref[i], jnp.float32) for i in range(4)]
    whole = raw[0] + raw[1] + raw[2] + raw[3]
    share = [value / whole for value in raw]
    row = lax.broadcasted_iota(jnp.int32, net_ref.shape[1:], 1)
    nets = []
    for k in range(3):
        net = net_ref[k]
        if k < 2:
            o = offset_ref[k]
            net = jnp.where(row >= o, pltpu.roll(net, o, 1), pltpu.roll(prev_ref[k], o, 1))
        nets.append((net[:, :, :cols], pltpu.roll(net, WINDOW - cols, 2)[:, :, :cols]))
    count = planes // 2
    for part in range(2):
        span = slice(part * count, (part + 1) * count)
        held = state_ref[0, 0, span]
        answer = fit_ref[0, span]
        joined = share[0] * (2.0 * answer - held)
        for k in range(3):
            joined = joined + share[k + 1] * (state_ref[k + 1, 0, span] - 2.0 * nets[k][part])
        next_ref[0, 0, span] = held + joined - answer
        for k in range(3):
            next_ref[k + 1, 0, span] = joined + nets[k][part]


VMEM = pl.BlockSpec(memory_space=pltpu.VMEM)
PARAMS = pltpu.CompilerParams(vmem_limit_bytes=20 * 1024 * 1024)
SMEM = pl.BlockSpec(memory_space=pltpu.SMEM)


def hop(value, axis, step):
    count = lax.axis_size(axis)
    return lax.ppermute(value, axis, [(i, (i + step) % count) for i in range(count)])


def step(
    agent_state, measured, bin_index, bin_frac, patch_offsets, agent_weights, up_weight, down_weight
):
    planes, row_count, col_count = agent_state.shape[2:]
    tile_count = lax.axis_size("tile")
    agent_count = lax.axis_size("agent")
    angles = bin_index.shape[0]
    pixels = row_count * col_count
    factor = 1.0 / math.sqrt(angles * (row_count * tile_count + col_count * agent_count))
    both = ("tile", "agent")
    f32 = jnp.float32

    shape = (planes // 2, row_count, 2 * col_count)
    head, tail = pl.pallas_call(
        pack_kernel,
        out_shape=[
            jax.ShapeDtypeStruct((2,) + shape, jnp.bfloat16),
            jax.ShapeDtypeStruct((1,) + shape, jnp.bfloat16),
        ],
        in_specs=[VMEM],
        out_specs=[VMEM] * 2,
        compiler_params=PARAMS,
        name="pack",
    )(agent_state)
    following = hop(head, "tile", -1)

    group = (lax.axis_index("tile") * agent_count // planes).astype(jnp.int32)
    pieces, flat, rel, near = pl.pallas_call(
        project_kernel,
        out_shape=[
            jax.ShapeDtypeStruct((2 * angles * planes, WINDOW), f32),
            jax.ShapeDtypeStruct((planes, pixels), f32),
            jax.ShapeDtypeStruct((angles, pixels), jnp.int32),
            jax.ShapeDtypeStruct((angles, pixels), f32),
        ],
        grid=(1,),
        in_specs=[
            SMEM,
            pl.BlockSpec((1,) + agent_state.shape[1:], lambda i: (0, 0, 0, 0, 0)),
            VMEM,
            VMEM,
            VMEM,
        ],
        out_specs=[VMEM] * 4,
        scratch_shapes=[pltpu.VMEM((angles, WINDOW), f32)],
        compiler_params=PARAMS,
        name="project",
    )(group.reshape(1), agent_state, bin_index, bin_frac, measured)

    region = pl.pallas_call(
        shift_kernel,
        out_shape=jax.ShapeDtypeStruct((3,) + shape, jnp.bfloat16),
        in_specs=[SMEM, VMEM, VMEM, VMEM],
        out_specs=VMEM,
        compiler_params=PARAMS,
        name="shift",
    )(patch_offsets, head, tail, following)
    region, pieces = lax.optimization_barrier((region, pieces))
    others = []
    for step in range(1, agent_count):
        others.append(hop(region, "agent", -step))

    count = angles * planes
    got = lax.all_to_all(pieces.reshape(count, 2, WINDOW), both, 0, 0, tiled=True)
    cut = pl.pallas_call(
        functools.partial(combine_kernel, factor, measured.shape[2]),
        out_shape=jax.ShapeDtypeStruct((angles * planes, WINDOW), f32),
        in_specs=[VMEM],
        out_specs=VMEM,
        compiler_params=PARAMS,
        name="combine",
    )(got.reshape(2 * count, WINDOW))

    parts = pl.pallas_call(
        denoise_kernel,
        out_shape=[jax.ShapeDtypeStruct((3,) + shape, f32)] * 4,
        in_specs=[SMEM] + [VMEM] * 6,
        out_specs=[VMEM] * 4,
        compiler_params=PARAMS,
        name="denoise",
    )(patch_offsets, region, *others, up_weight, down_weight)
    arrived = []
    for step in range(1, agent_count):
        arrived.append(hop(parts[step], "agent", step))

    back = lax.all_to_all(cut, both, 0, 0, tiled=True)
    nets = parts[0] + arrived[0] + arrived[1] + arrived[2]
    previous = hop(nets[:2], "tile", 1)

    return pl.pallas_call(
        functools.partial(finish_kernel, factor),
        out_shape=[
            jax.ShapeDtypeStruct(agent_state.shape, f32),
            jax.ShapeDtypeStruct(agent_state.shape[1:], f32),
        ],
        in_specs=[SMEM, SMEM] + [VMEM] * 7,
        out_specs=[VMEM, VMEM],
        compiler_params=PARAMS,
        name="finish",
    )(
        patch_offsets, agent_weights, agent_state, flat, rel, near,
        back.reshape(angles, planes, WINDOW), nets, previous,
    )


def solution(mesh):
    placed = (
        P(None, None, None, "tile", "agent"),
        P(None, None, ("tile", "agent")),
        P(None, "tile", "agent"),
        P(None, "tile", "agent"),
        P(),
        P(),
        P(None, None, "agent"),
        P(None, "agent", None),
    )
    return jax.shard_map(
        step,
        mesh=mesh,
        in_specs=placed,
        out_specs=(P(None, None, None, "tile", "agent"), P(None, None, "tile", "agent")),
        check_vma=False,
    )
```

```python
import functools
import math

import jax
import jax.numpy as jnp
from jax import lax
from jax.experimental import pallas as pl
from jax.experimental.pallas import tpu as pltpu
from jax.sharding import PartitionSpec as P


PATCH = 16
SCALE = 724
WINDOW = 128
ALIGN = 32


def split_two(value):
    high = value.astype(jnp.bfloat16)
    return high, (value - high.astype(jnp.float32)).astype(jnp.bfloat16)


def window_starts(low):
    return (jnp.min(low, axis=1, keepdims=True) // ALIGN) * ALIGN


def one_hot(rel_row):
    spots = lax.broadcasted_iota(jnp.int32, (WINDOW, rel_row.shape[1]), 0)
    return jnp.where(spots == rel_row, 1.0, 0.0).astype(jnp.bfloat16)


def project_kernel(
    group_ref, state_hbm, bin_hbm, num_hbm, meas_hbm, out_ref, u_ref, rel_ref, w_ref, start_ref,
    state_ref, bin_ref, num_ref, meas_ref, sems,
):
    loads = [
        pltpu.make_async_copy(state_hbm.at[0, 0], state_ref, sems.at[0]),
        pltpu.make_async_copy(bin_hbm, bin_ref, sems.at[1]),
        pltpu.make_async_copy(num_hbm, num_ref, sems.at[2]),
        pltpu.make_async_copy(meas_hbm.at[0], meas_ref, sems.at[3]),
    ]
    for load in loads:
        load.start()
    out_ref[...] = jnp.zeros_like(out_ref)
    for load in loads:
        load.wait()
    angles, rows, cols = bin_ref.shape
    planes = state_ref.shape[0]
    for x in range(rows):
        span = slice(x * cols, (x + 1) * cols)
        u_ref[:, span] = state_ref[:, x, :]
        rel_ref[:, span] = bin_ref[:, x, :]
        w_ref[:, span] = num_ref[:, x, :].astype(jnp.float32) * (1.0 / SCALE)
    low = rel_ref[...]
    start = window_starts(low)
    rel_ref[...] = low - start
    start_ref[...] = jnp.broadcast_to(start.astype(jnp.float32), (angles, WINDOW))
    owned = meas_ref.shape[1]
    mine = pl.multiple_of(group_ref[0] * (2 * planes), 2 * planes)
    out_ref[pl.ds(mine + 1, planes, stride=2), :owned] = meas_ref[...]
    lane = lax.broadcasted_iota(jnp.int32, (planes, WINDOW), 1)

    def body(a, carry):
        band = one_hot(rel_ref[pl.ds(a, 1), :])
        u = u_ref[...]
        near = u * w_ref[pl.ds(a, 1), :]
        near_hi, near_lo = split_two(near)
        far_hi, far_lo = split_two(u - near)
        terms = jnp.concatenate([near_hi, near_lo, far_hi, far_lo], axis=0)
        sums = lax.dot_general(
            terms, band, (((1,), (1,)), ((), ())), preferred_element_type=jnp.float32
        )
        at_low = sums[:planes] + sums[planes : 2 * planes]
        above = sums[2 * planes : 3 * planes] + sums[3 * planes :]
        piece = at_low + pltpu.roll(above, 1, 1)
        piece = jnp.where(lane == WINDOW - 1, start_ref[pl.ds(a, 1), :], piece)
        first = pl.multiple_of(a * (2 * planes), 2 * planes)
        out_ref[pl.ds(first, planes, stride=2), :] = piece
        return carry

    lax.fori_loop(0, angles, body, 0, unroll=2)


def combine_kernel(factor, owned, got_ref, out_ref):
    count = got_ref.shape[0] // 2
    step = WINDOW // ALIGN
    rows = 16
    got = got_ref[pl.ds(0, count, stride=2), :]
    lane_all = lax.broadcasted_iota(jnp.int32, (count, WINDOW), 1)
    piece = jnp.where(lane_all < WINDOW - 1, got, 0.0)
    block = got[:, WINDOW - 1 :].astype(jnp.int32) // ALIGN
    slot = (block % step) * rows + block // step
    slots = lax.broadcasted_iota(jnp.int32, (count, step * rows), 1)
    route = jnp.where(slots == slot, 1.0, 0.0).astype(jnp.bfloat16)
    sums = lax.dot_general(
        route,
        jnp.concatenate(split_two(piece), axis=1),
        (((0,), (0,)), ((), ())),
        preferred_element_type=jnp.float32,
    )
    sums = sums[:, :WINDOW] + sums[:, WINDOW:]
    lane = lax.broadcasted_iota(jnp.int32, (rows, WINDOW), 1)
    row = lax.broadcasted_iota(jnp.int32, (rows, WINDOW), 0)
    sino = sums[:rows]
    for m in range(1, step):
        turned = pltpu.roll(sums[m * rows : (m + 1) * rows], m * ALIGN, 1)
        here = lane >= m * ALIGN
        sino = sino + jnp.where(here, turned, 0.0)
        sino = sino + pltpu.roll(jnp.where(here, 0.0, turned), 1, 0)
    sent = got_ref[pl.ds(1, count, stride=2), :]
    taken = jnp.sum(sent.reshape(count // 16, 16, WINDOW), axis=0)
    taken = jnp.where(lax.broadcasted_iota(jnp.int32, taken.shape, 1) < owned, taken, 0.0)
    target = jnp.zeros_like(sino)
    for i in range(16):
        first, off = divmod(i * owned, WINDOW)
        turned = taken[i : i + 1]
        if off:
            turned = pltpu.roll(turned, off, 1)
        hit = ((row == first) & (lane >= off)) | ((row == first + 1) & (lane < off))
        target = target + jnp.where(hit, turned, 0.0)
    misfit = factor * sino - target
    views = [misfit]
    for m in range(1, step):
        turned = pltpu.roll(misfit, WINDOW - m * ALIGN, 1)
        views.append(
            jnp.where(lane < WINDOW - m * ALIGN, turned, pltpu.roll(turned, rows - 1, 0))
        )
    views = jnp.concatenate(views, axis=0)
    cut = jnp.dot(
        route, jnp.concatenate(split_two(views), axis=1), preferred_element_type=jnp.float32
    )
    out_ref[...] = cut[:, :WINDOW] + cut[:, WINDOW:]


def pack_kernel(offset_ref, state_hbm, keep_ref, send_ref, state_ref, sem):
    load = pltpu.make_async_copy(state_hbm.at[pl.ds(1, 3), 0], state_ref, sem)
    load.start()
    load.wait()
    half, rows, cols = state_ref.shape[1] // 2, state_ref.shape[2], state_ref.shape[3]
    row = lax.broadcasted_iota(jnp.int32, (half, rows, cols), 1)
    for k in range(3):
        for part in range(2):
            block = state_ref[k, part * half : (part + 1) * half]
            span = slice(part * cols, (part + 1) * cols)
            if k == 2:
                keep_ref[k, :, :, span] = block.astype(keep_ref.dtype)
                continue
            o = offset_ref[k]
            block = pltpu.roll(block, rows - o, 1)
            own = row < rows - o
            keep_ref[k, :, :, span] = jnp.where(own, block, 0.0).astype(keep_ref.dtype)
            send_ref[k, :, :, span] = jnp.where(own, 0.0, block).astype(send_ref.dtype)


def shift_kernel(keep_ref, next_ref, out_ref):
    out_ref[:2] = keep_ref[:2] + next_ref[...]
    out_ref[2] = keep_ref[2]


def add_kernel(p0, p1, p2, p3, head_ref, tail_ref):
    total = p0[...] + p1[...] + p2[...] + p3[...]
    head_ref[...] = total[:2]
    tail_ref[...] = total[2:]


def swap_slabs(slabs):
    lane = lax.broadcasted_iota(jnp.int32, slabs[0].shape, 1)
    width = slabs[0].shape[1]
    slabs = list(slabs)
    for step in (1, 2, 4, 8):
        odd = (lane & step) != 0
        for i in range(len(slabs)):
            if i & step:
                continue
            first, second = slabs[i], slabs[i + step]
            slabs[i] = jnp.where(odd, pltpu.roll(second, step, 1), first)
            slabs[i + step] = jnp.where(odd, second, pltpu.roll(first, width - step, 1))
    return slabs


def swap_rows(slab):
    width = slab.shape[1]
    top, low = slab[:8], slab[8:]
    lane = lax.broadcasted_iota(jnp.int32, top.shape, 1)
    row = lax.broadcasted_iota(jnp.int32, top.shape, 0)
    odd = (lane & 8) != 0
    top, low = (
        jnp.where(odd, pltpu.roll(low, 8, 1), top),
        jnp.where(odd, low, pltpu.roll(top, width - 8, 1)),
    )
    halves = []
    for half in (top, low):
        for step in (1, 2, 4):
            odd_lane, odd_row = (lane & step) != 0, (row & step) != 0
            up = pltpu.roll(pltpu.roll(half, 8 - step, 0), step, 1)
            down = pltpu.roll(pltpu.roll(half, step, 0), width - step, 1)
            other = jnp.where(odd_lane, up, down)
            half = jnp.where(odd_lane == odd_row, half, other)
        halves.append(half)
    return jnp.concatenate(halves, axis=0)


def denoise_kernel(
    offset_ref, p0, p1, p2, p3, up_hbm, down_hbm, o0, o1, o2, o3, up_ref, down_ref, sems
):
    loads = []
    for k in range(3):
        up = pltpu.make_async_copy(up_hbm.at[k], up_ref.at[k], sems.at[k])
        down = pltpu.make_async_copy(down_hbm.at[k], down_ref.at[k], sems.at[3 + k])
        up.start()
        down.start()
        loads.append((up, down))
    side = PATCH
    size = side * side
    row = lax.broadcasted_iota(jnp.int32, (size, size), 0)
    col = lax.broadcasted_iota(jnp.int32, (size, size), 1)
    turned = (row % side) * side + row // side
    exchange = jnp.where(col == turned, 1.0, 0.0).astype(jnp.bfloat16)
    lane = lax.broadcasted_iota(jnp.int32, (size // 2, WINDOW), 1)
    left = lane < WINDOW // 2
    wide = lax.broadcasted_iota(jnp.int32, (size, WINDOW), 1)

    def joined(a, b):
        a = a.reshape(size // 2, WINDOW).astype(jnp.float32)
        b = b.reshape(size // 2, WINDOW).astype(jnp.float32)
        early = jnp.where(left, a, pltpu.roll(b, WINDOW // 2, 1))
        late = jnp.where(left, pltpu.roll(a, WINDOW // 2, 1), b)
        return jnp.concatenate([early, late], axis=0)

    def slabs_of(half):
        return [half[i * side : (i + 1) * side] for i in range(side)]

    def arrange(which, half):
        if which == 0:
            return jnp.concatenate(swap_slabs(slabs_of(half)), axis=0)
        if which == 2:
            return jnp.concatenate([swap_rows(slab) for slab in slabs_of(half)], axis=0)
        return half

    for k in range(3):
        halves = [joined(p0[k], p1[k]), joined(p2[k], p3[k])]
        if k != 1:
            o = offset_ref[k]
            a, b = [pltpu.roll(half, WINDOW - o, 1) for half in halves]
            inside = wide < WINDOW - o
            halves = [jnp.where(inside, a, b), jnp.where(inside, b, a)]
        halves = [arrange(k, half) for half in halves]
        patches = jnp.concatenate([half.T for half in halves], axis=0).astype(jnp.bfloat16)
        for load in loads[k]:
            load.wait()
        down = down_ref[k]
        if k == 0:
            patches = jnp.dot(
                patches, exchange, preferred_element_type=jnp.float32
            ).astype(jnp.bfloat16)
            down = jnp.dot(down, exchange, preferred_element_type=jnp.float32).astype(jnp.bfloat16)
        hidden = jnp.dot(patches, up_ref[k], preferred_element_type=jnp.float32)
        hidden = jnp.maximum(hidden, 0.0).astype(jnp.bfloat16)
        result = jnp.dot(hidden, down, preferred_element_type=jnp.float32)
        halves = [arrange(k, result[:WINDOW].T), arrange(k, result[WINDOW:].T)]
        if k != 1:
            a, b = [pltpu.roll(half, o, 1) for half in halves]
            inside = wide >= o
            halves = [jnp.where(inside, a, b), jnp.where(inside, b, a)]
        for half, first, second in ((halves[0], o0, o1), (halves[1], o2, o3)):
            early, late = half[: size // 2], half[size // 2 :]
            first[k] = jnp.where(left, early, pltpu.roll(late, WINDOW // 2, 1)).reshape(
                first.shape[1:]
            )
            second[k] = jnp.where(left, pltpu.roll(early, WINDOW // 2, 1), late).reshape(
                second.shape[1:]
            )


def spread_kernel(factor, u_ref, rel_ref, w_ref, win_ref, fit_ref, copy_ref):
    angles, planes, _ = win_ref.shape

    def body(a, total):
        band = one_hot(rel_ref[pl.ds(a, 1), :])
        at_low = win_ref[a]
        above = pltpu.roll(at_low, WINDOW - 1, 1)
        terms = jnp.concatenate(split_two(at_low) + split_two(above), axis=0)
        picked = jnp.dot(terms, band, preferred_element_type=jnp.float32)
        near = picked[:planes] + picked[planes : 2 * planes]
        far = picked[2 * planes : 3 * planes] + picked[3 * planes :]
        w = w_ref[pl.ds(a, 1), :]
        return total + (far + w * (near - far))

    total = lax.fori_loop(0, angles, body, jnp.zeros(u_ref.shape, jnp.float32), unroll=2)
    fit = u_ref[...] - factor * total
    rows, cols = fit_ref.shape[2:]
    for x in range(rows):
        fit_ref[0, :, x, :] = fit[:, x * cols : (x + 1) * cols]
    copy_ref[...] = fit_ref[...]


def join_kernel(
    offset_ref, weight_ref, state_ref, fit_ref, head_ref, tail_ref, prev_ref, next_ref
):
    planes, _, cols = fit_ref.shape[1:]
    raw = [jnp.full((1, cols), weight_ref[i], jnp.float32) for i in range(4)]
    whole = raw[0] + raw[1] + raw[2] + raw[3]
    share = [value / whole for value in raw]
    row = lax.broadcasted_iota(jnp.int32, tail_ref.shape[1:], 1)
    nets = []
    for k in range(3):
        if k == 2:
            net = tail_ref[0]
        else:
            net, o = head_ref[k], offset_ref[k]
            net = jnp.where(row >= o, pltpu.roll(net, o, 1), pltpu.roll(prev_ref[k], o, 1))
        nets.append((net[:, :, :cols], pltpu.roll(net, WINDOW - cols, 2)[:, :, :cols]))
    count = planes // 2
    for part in range(2):
        span = slice(part * count, (part + 1) * count)
        held = state_ref[0, 0, span]
        answer = fit_ref[0, span]
        joined = share[0] * (2.0 * answer - held)
        for k in range(3):
            joined = joined + share[k + 1] * (state_ref[k + 1, 0, span] - 2.0 * nets[k][part])
        next_ref[0, 0, span] = held + joined - answer
        for k in range(3):
            next_ref[k + 1, 0, span] = joined + nets[k][part]


VMEM = pl.BlockSpec(memory_space=pltpu.VMEM)
PARAMS = pltpu.CompilerParams(vmem_limit_bytes=20 * 1024 * 1024)
HBM = pl.BlockSpec(memory_space=pltpu.HBM)
SMEM = pl.BlockSpec(memory_space=pltpu.SMEM)


def cost(micros):
    return pl.CostEstimate(flops=micros * 10**9, bytes_accessed=micros * 3 * 10**6, transcendentals=0)


def hop(value, axis, step):
    count = lax.axis_size(axis)
    return lax.ppermute(value, axis, [(i, (i + step) % count) for i in range(count)])


def step(
    agent_state, measured, bin_index, bin_frac, patch_offsets, agent_weights, up_weight, down_weight
):
    planes, row_count, col_count = agent_state.shape[2:]
    tile_count = lax.axis_size("tile")
    agent_count = lax.axis_size("agent")
    angles = bin_index.shape[0]
    pixels = row_count * col_count
    factor = 1.0 / math.sqrt(angles * (row_count * tile_count + col_count * agent_count))
    both = ("tile", "agent")
    f32 = jnp.float32

    shape = (planes // 2, row_count, 2 * col_count)
    keep, sent = pl.pallas_call(
        pack_kernel,
        out_shape=[
            jax.ShapeDtypeStruct((3,) + shape, jnp.bfloat16),
            jax.ShapeDtypeStruct((2,) + shape, jnp.bfloat16),
        ],
        in_specs=[SMEM, HBM],
        out_specs=[VMEM] * 2,
        scratch_shapes=[
            pltpu.VMEM((3,) + agent_state.shape[2:], f32),
            pltpu.SemaphoreType.DMA(()),
        ],
        compiler_params=pltpu.CompilerParams(vmem_limit_bytes=56050000),
        cost_estimate=cost(2),
        name="pack",
    )(patch_offsets, agent_state)
    following = hop(sent, "tile", -1)

    group = (lax.axis_index("tile") * agent_count // planes).astype(jnp.int32)
    pieces, flat, rel, near = pl.pallas_call(
        project_kernel,
        out_shape=[
            jax.ShapeDtypeStruct((2 * angles * planes, WINDOW), f32),
            jax.ShapeDtypeStruct((planes, pixels), f32),
            jax.ShapeDtypeStruct((angles, pixels), jnp.int32),
            jax.ShapeDtypeStruct((angles, pixels), f32),
        ],
        in_specs=[SMEM] + [HBM] * 4,
        out_specs=[VMEM] * 4,
        scratch_shapes=[
            pltpu.VMEM((angles, WINDOW), f32),
            pltpu.VMEM(agent_state.shape[2:], f32),
            pltpu.VMEM(bin_index.shape, jnp.int32),
            pltpu.VMEM(bin_frac.shape, jnp.int32),
            pltpu.VMEM(measured.shape[1:], f32),
            pltpu.SemaphoreType.DMA((4,)),
        ],
        compiler_params=pltpu.CompilerParams(vmem_limit_bytes=56250000),
        cost_estimate=cost(5),
        name="project",
    )(group.reshape(1), agent_state, bin_index, bin_frac, measured)

    region = pl.pallas_call(
        shift_kernel,
        out_shape=jax.ShapeDtypeStruct((3,) + shape, jnp.bfloat16),
        in_specs=[VMEM, VMEM],
        out_specs=VMEM,
        compiler_params=PARAMS,
        cost_estimate=cost(1),
        name="shift",
    )(keep, following)
    others = []
    for step in range(1, agent_count):
        others.append(hop(region, "agent", -step))

    count = angles * planes
    got = lax.all_to_all(pieces.reshape(count, 2, WINDOW), both, 0, 0, tiled=True)
    cut = pl.pallas_call(
        functools.partial(combine_kernel, factor, measured.shape[2]),
        out_shape=jax.ShapeDtypeStruct((angles * planes, WINDOW), f32),
        in_specs=[VMEM],
        out_specs=VMEM,
        compiler_params=PARAMS,
        cost_estimate=cost(2),
        name="combine",
    )(got.reshape(2 * count, WINDOW))

    back = lax.all_to_all(cut, both, 0, 0, tiled=True)
    parts = pl.pallas_call(
        denoise_kernel,
        out_shape=[jax.ShapeDtypeStruct((3,) + shape, f32)] * 4,
        in_specs=[SMEM] + [VMEM] * 4 + [HBM] * 2,
        out_specs=[VMEM] * 4,
        scratch_shapes=[
            pltpu.VMEM(up_weight.shape, up_weight.dtype),
            pltpu.VMEM(down_weight.shape, down_weight.dtype),
            pltpu.SemaphoreType.DMA((6,)),
        ],
        compiler_params=pltpu.CompilerParams(vmem_limit_bytes=54500000),
        cost_estimate=cost(6),
        name="denoise",
    )(patch_offsets, region, *others, up_weight, down_weight)
    arrived = []
    for step in range(1, agent_count):
        arrived.append(hop(parts[step], "agent", step))

    fit, held = pl.pallas_call(
        functools.partial(spread_kernel, factor),
        out_shape=[jax.ShapeDtypeStruct(agent_state.shape[1:], f32)] * 2,
        in_specs=[VMEM] * 4,
        out_specs=[VMEM] * 2,
        compiler_params=PARAMS,
        cost_estimate=cost(4),
        name="spread",
    )(flat, rel, near, back.reshape(angles, planes, WINDOW))
    head, tail = pl.pallas_call(
        add_kernel,
        out_shape=[
            jax.ShapeDtypeStruct((2,) + shape, f32),
            jax.ShapeDtypeStruct((1,) + shape, f32),
        ],
        in_specs=[VMEM] * 4,
        out_specs=[VMEM] * 2,
        compiler_params=PARAMS,
        cost_estimate=cost(1),
        name="add",
    )(parts[0], *arrived)
    previous = hop(head, "tile", 1)
    state_next = pl.pallas_call(
        join_kernel,
        out_shape=jax.ShapeDtypeStruct(agent_state.shape, f32),
        in_specs=[SMEM, SMEM] + [VMEM] * 5,
        out_specs=VMEM,
        compiler_params=PARAMS,
        cost_estimate=cost(2),
        name="join",
    )(patch_offsets, agent_weights, agent_state, held, head, tail, previous)
    return (state_next, fit)


def solution(mesh):
    placed = (
        P(None, None, None, "tile", "agent"),
        P(None, None, ("tile", "agent")),
        P(None, "tile", "agent"),
        P(None, "tile", "agent"),
        P(),
        P(),
        P(None, None, "agent"),
        P(None, "agent", None),
    )
    return jax.shard_map(
        step,
        mesh=mesh,
        in_specs=placed,
        out_specs=(P(None, None, None, "tile", "agent"), P(None, None, "tile", "agent")),
        check_vma=False,
    )
```

```python
import functools
import math

import jax
import jax.numpy as jnp
from jax import lax
from jax.experimental import pallas as pl
from jax.experimental.pallas import tpu as pltpu
from jax.sharding import PartitionSpec as P


PATCH = 16
SCALE = 724
WINDOW = 128
ALIGN = 32
WIRE = jnp.int16
STEPS = 32700.0
GRAIN = 128.0


def split_two(value):
    high = value.astype(jnp.bfloat16)
    return high, (value - high.astype(jnp.float32)).astype(jnp.bfloat16)


def window_starts(low):
    return (jnp.min(low, axis=1, keepdims=True) // ALIGN) * ALIGN


def one_hot(rel_row):
    spots = lax.broadcasted_iota(jnp.int32, (WINDOW, rel_row.shape[1]), 0)
    return jnp.where(spots == rel_row, 1.0, 0.0).astype(jnp.bfloat16)


def project_kernel(
    group_ref, state_ref, bin_ref, num_ref, meas_ref, out_ref, u_ref, rel_ref, w_ref, start_ref
):
    out_ref[...] = jnp.zeros_like(out_ref)
    angles, rows, cols = bin_ref.shape
    planes = state_ref.shape[0]
    for x in range(rows):
        span = slice(x * cols, (x + 1) * cols)
        u_ref[:, span] = state_ref[:, x, :]
        rel_ref[:, span] = bin_ref[:, x, :]
        w_ref[:, span] = num_ref[:, x, :].astype(jnp.float32) * (1.0 / SCALE)
    low = rel_ref[...]
    start = window_starts(low)
    rel_ref[...] = low - start
    start_ref[...] = jnp.broadcast_to(start.astype(jnp.float32), (angles, WINDOW))
    owned = meas_ref.shape[2]
    mine = pl.multiple_of(group_ref[0] * (2 * planes), 2 * planes)
    out_ref[pl.ds(mine + 1, planes, stride=2), :owned] = meas_ref[0]
    lane = lax.broadcasted_iota(jnp.int32, (planes, WINDOW), 1)

    def body(a, carry):
        band = one_hot(rel_ref[pl.ds(a, 1), :])
        u = u_ref[...]
        near = u * w_ref[pl.ds(a, 1), :]
        near_hi, near_lo = split_two(near)
        far_hi, far_lo = split_two(u - near)
        terms = jnp.concatenate([near_hi, near_lo, far_hi, far_lo], axis=0)
        sums = lax.dot_general(
            terms, band, (((1,), (1,)), ((), ())), preferred_element_type=jnp.float32
        )
        at_low = sums[:planes] + sums[planes : 2 * planes]
        above = sums[2 * planes : 3 * planes] + sums[3 * planes :]
        piece = at_low + pltpu.roll(above, 1, 1)
        piece = jnp.where(lane == WINDOW - 1, start_ref[pl.ds(a, 1), :], piece)
        first = pl.multiple_of(a * (2 * planes), 2 * planes)
        out_ref[pl.ds(first, planes, stride=2), :] = piece
        return carry

    lax.fori_loop(0, angles, body, 0, unroll=8)


def combine_kernel(factor, owned, got_ref, out_ref):
    count = got_ref.shape[0] // 2
    step = WINDOW // ALIGN
    rows = 16
    got = got_ref[pl.ds(0, count, stride=2), :]
    lane_all = lax.broadcasted_iota(jnp.int32, (count, WINDOW), 1)
    piece = jnp.where(lane_all < WINDOW - 1, got, 0.0)
    block = got[:, WINDOW - 1 :].astype(jnp.int32) // ALIGN
    slot = (block % step) * rows + block // step
    slots = lax.broadcasted_iota(jnp.int32, (count, step * rows), 1)
    route = jnp.where(slots == slot, 1.0, 0.0).astype(jnp.bfloat16)
    sums = lax.dot_general(
        route,
        jnp.concatenate(split_two(piece), axis=1),
        (((0,), (0,)), ((), ())),
        preferred_element_type=jnp.float32,
    )
    sums = sums[:, :WINDOW] + sums[:, WINDOW:]
    lane = lax.broadcasted_iota(jnp.int32, (rows, WINDOW), 1)
    row = lax.broadcasted_iota(jnp.int32, (rows, WINDOW), 0)
    sino = sums[:rows]
    for m in range(1, step):
        turned = pltpu.roll(sums[m * rows : (m + 1) * rows], m * ALIGN, 1)
        here = lane >= m * ALIGN
        sino = sino + jnp.where(here, turned, 0.0)
        sino = sino + pltpu.roll(jnp.where(here, 0.0, turned), 1, 0)
    sent = got_ref[pl.ds(1, count, stride=2), :]
    taken = jnp.sum(sent.reshape(count // 16, 16, WINDOW), axis=0)
    taken = jnp.where(lax.broadcasted_iota(jnp.int32, taken.shape, 1) < owned, taken, 0.0)
    target = jnp.zeros_like(sino)
    for i in range(16):
        first, off = divmod(i * owned, WINDOW)
        turned = taken[i : i + 1]
        if off:
            turned = pltpu.roll(turned, off, 1)
        hit = ((row == first) & (lane >= off)) | ((row == first + 1) & (lane < off))
        target = target + jnp.where(hit, turned, 0.0)
    misfit = factor * sino - target
    views = [misfit]
    for m in range(1, step):
        turned = pltpu.roll(misfit, WINDOW - m * ALIGN, 1)
        views.append(
            jnp.where(lane < WINDOW - m * ALIGN, turned, pltpu.roll(turned, rows - 1, 0))
        )
    views = jnp.concatenate(views, axis=0)
    cut = jnp.dot(
        route, jnp.concatenate(split_two(views), axis=1), preferred_element_type=jnp.float32
    )
    out_ref[...] = cut[:, :WINDOW] + cut[:, WINDOW:]


def pack_kernel(
    state_hbm, bin_hbm, num_hbm, head_ref, tail_ref, first_ref, bin_ref, num_ref, state_ref, sems
):
    load = pltpu.make_async_copy(state_hbm.at[pl.ds(1, 3), 0], state_ref, sems.at[0])
    ahead = [
        pltpu.make_async_copy(state_hbm.at[0, 0], first_ref, sems.at[1]),
        pltpu.make_async_copy(bin_hbm, bin_ref, sems.at[2]),
        pltpu.make_async_copy(num_hbm, num_ref, sems.at[3]),
    ]
    for copy in [load] + ahead:
        copy.start()
    load.wait()
    half, cols = state_ref.shape[1] // 2, state_ref.shape[3]
    for k in range(3):
        out = head_ref.at[k] if k < 2 else tail_ref.at[0]
        for part in range(2):
            block = state_ref[k, part * half : (part + 1) * half]
            out[:, :, part * cols : (part + 1) * cols] = block.astype(out.dtype)
    for copy in ahead:
        copy.wait()


def shift_kernel(offset_ref, head_ref, tail_ref, next_ref, out_ref):
    rows = head_ref.shape[2]
    for k in range(2):
        o = offset_ref[k]
        own = pltpu.roll(head_ref[k].astype(jnp.float32), rows - o, 1)
        more = pltpu.roll(next_ref[k].astype(jnp.float32), rows - o, 1)
        row = lax.broadcasted_iota(jnp.int32, own.shape, 1)
        out_ref[k] = jnp.where(row < rows - o, own, more).astype(out_ref.dtype)
    out_ref[2] = tail_ref[0]


def encode(block, out):
    count = block.shape[0]
    top = jnp.max(jnp.max(jnp.abs(block), axis=0), axis=0, keepdims=True)
    level = jnp.ceil(jnp.log2(jnp.maximum(top, 1e-30)) * GRAIN)
    scale = STEPS * jnp.exp2(level * (-1.0 / GRAIN))
    out[:count] = jnp.round(block * scale[None]).astype(jnp.int32).astype(out.dtype)
    level = jnp.broadcast_to(level, block.shape[1:])
    out[count] = level.astype(jnp.int32).astype(out.dtype)


def decode(held):
    count = held.shape[0] - 1
    level = held[count].astype(jnp.float32)[:1]
    scale = (1.0 / STEPS) * jnp.exp2(level * (1.0 / GRAIN))
    return held[:count].astype(jnp.float32) * scale[None]


def halve_kernel(near_ref, got_ref, keep_ref, send_ref):
    for k in range(3):
        keep_ref[k] = near_ref[0, k] + decode(got_ref.at[0, k])
        encode(near_ref[1, k] + decode(got_ref.at[1, k]), send_ref.at[k])


def add_kernel(keep_ref, got_ref, head_ref, tail_ref):
    for k in range(3):
        out = head_ref.at[k] if k < 2 else tail_ref.at[0]
        out[...] = keep_ref[k] + decode(got_ref.at[k])


def swap_slabs(slabs):
    lane = lax.broadcasted_iota(jnp.int32, slabs[0].shape, 1)
    width = slabs[0].shape[1]
    slabs = list(slabs)
    for step in (1, 2, 4, 8):
        odd = (lane & step) != 0
        for i in range(len(slabs)):
            if i & step:
                continue
            first, second = slabs[i], slabs[i + step]
            slabs[i] = jnp.where(odd, pltpu.roll(second, step, 1), first)
            slabs[i + step] = jnp.where(odd, second, pltpu.roll(first, width - step, 1))
    return slabs


def swap_rows(slab):
    width = slab.shape[1]
    top, low = slab[:8], slab[8:]
    lane = lax.broadcasted_iota(jnp.int32, top.shape, 1)
    row = lax.broadcasted_iota(jnp.int32, top.shape, 0)
    odd = (lane & 8) != 0
    top, low = (
        jnp.where(odd, pltpu.roll(low, 8, 1), top),
        jnp.where(odd, low, pltpu.roll(top, width - 8, 1)),
    )
    halves = []
    for half in (top, low):
        for step in (1, 2, 4):
            odd_lane, odd_row = (lane & step) != 0, (row & step) != 0
            up = pltpu.roll(pltpu.roll(half, 8 - step, 0), step, 1)
            down = pltpu.roll(pltpu.roll(half, step, 0), width - step, 1)
            other = jnp.where(odd_lane, up, down)
            half = jnp.where(odd_lane == odd_row, half, other)
        halves.append(half)
    return jnp.concatenate(halves, axis=0)


def denoise_kernel(
    offset_ref, p0, p1, p2, p3, up_hbm, down_hbm, near_ref, far_ref, up_ref, down_ref, sems
):
    loads = []
    for k in range(3):
        up = pltpu.make_async_copy(up_hbm.at[k], up_ref.at[k], sems.at[k])
        down = pltpu.make_async_copy(down_hbm.at[k], down_ref.at[k], sems.at[3 + k])
        up.start()
        down.start()
        loads.append((up, down))
    side = PATCH
    size = side * side
    row = lax.broadcasted_iota(jnp.int32, (size, size), 0)
    col = lax.broadcasted_iota(jnp.int32, (size, size), 1)
    turned = (row % side) * side + row // side
    exchange = jnp.where(col == turned, 1.0, 0.0).astype(jnp.bfloat16)
    lane = lax.broadcasted_iota(jnp.int32, (size // 2, WINDOW), 1)
    left = lane < WINDOW // 2
    wide = lax.broadcasted_iota(jnp.int32, (size, WINDOW), 1)

    def joined(a, b):
        a = a.reshape(size // 2, WINDOW).astype(jnp.float32)
        b = b.reshape(size // 2, WINDOW).astype(jnp.float32)
        early = jnp.where(left, a, pltpu.roll(b, WINDOW // 2, 1))
        late = jnp.where(left, pltpu.roll(a, WINDOW // 2, 1), b)
        return jnp.concatenate([early, late], axis=0)

    def slabs_of(half):
        return [half[i * side : (i + 1) * side] for i in range(side)]

    def arrange(which, half):
        if which == 0:
            return jnp.concatenate(swap_slabs(slabs_of(half)), axis=0)
        if which == 2:
            return jnp.concatenate([swap_rows(slab) for slab in slabs_of(half)], axis=0)
        return half

    for k in range(3):
        halves = [joined(p0[k], p1[k]), joined(p2[k], p3[k])]
        if k != 1:
            o = offset_ref[k]
            a, b = [pltpu.roll(half, WINDOW - o, 1) for half in halves]
            inside = wide < WINDOW - o
            halves = [jnp.where(inside, a, b), jnp.where(inside, b, a)]
        halves = [arrange(k, half) for half in halves]
        patches = jnp.concatenate([half.T for half in halves], axis=0).astype(jnp.bfloat16)
        for load in loads[k]:
            load.wait()
        down = down_ref[k]
        if k == 0:
            patches = jnp.dot(
                patches, exchange, preferred_element_type=jnp.float32
            ).astype(jnp.bfloat16)
            down = jnp.dot(down, exchange, preferred_element_type=jnp.float32).astype(jnp.bfloat16)
        hidden = jnp.dot(patches, up_ref[k], preferred_element_type=jnp.float32)
        hidden = jnp.maximum(hidden, 0.0).astype(jnp.bfloat16)
        result = jnp.dot(hidden, down, preferred_element_type=jnp.float32)
        halves = [arrange(k, result[:WINDOW].T), arrange(k, result[WINDOW:].T)]
        if k != 1:
            a, b = [pltpu.roll(half, o, 1) for half in halves]
            inside = wide >= o
            halves = [jnp.where(inside, a, b), jnp.where(inside, b, a)]
        for half, near in ((halves[0], True), (halves[1], False)):
            early, late = half[: size // 2], half[size // 2 :]
            blocks = (
                jnp.where(left, early, pltpu.roll(late, WINDOW // 2, 1)),
                jnp.where(left, pltpu.roll(early, WINDOW // 2, 1), late),
            )
            for j in range(2):
                block = blocks[j].reshape(near_ref.shape[2:])
                if near:
                    near_ref[j, k] = block
                else:
                    encode(block, far_ref.at[j, k])


def spread_kernel(factor, u_ref, rel_ref, w_ref, win_ref, fit_ref, copy_ref):
    angles, planes, _ = win_ref.shape

    def body(a, total):
        band = one_hot(rel_ref[pl.ds(a, 1), :])
        at_low = win_ref[a]
        above = pltpu.roll(at_low, WINDOW - 1, 1)
        terms = jnp.concatenate(split_two(at_low) + split_two(above), axis=0)
        picked = jnp.dot(terms, band, preferred_element_type=jnp.float32)
        near = picked[:planes] + picked[planes : 2 * planes]
        far = picked[2 * planes : 3 * planes] + picked[3 * planes :]
        w = w_ref[pl.ds(a, 1), :]
        return total + (far + w * (near - far))

    total = lax.fori_loop(0, angles, body, jnp.zeros(u_ref.shape, jnp.float32), unroll=8)
    fit = u_ref[...] - factor * total
    rows, cols = fit_ref.shape[2:]
    for x in range(rows):
        fit_ref[0, :, x, :] = fit[:, x * cols : (x + 1) * cols]
    copy_ref[...] = fit_ref[...]


def join_kernel(
    offset_ref, weight_ref, state_ref, fit_ref, head_ref, tail_ref, prev_ref, next_ref
):
    planes, _, cols = fit_ref.shape[1:]
    raw = [jnp.full((1, cols), weight_ref[i], jnp.float32) for i in range(4)]
    whole = raw[0] + raw[1] + raw[2] + raw[3]
    share = [value / whole for value in raw]
    row = lax.broadcasted_iota(jnp.int32, tail_ref.shape[1:], 1)
    nets = []
    for k in range(3):
        if k == 2:
            net = tail_ref[0]
        else:
            net, o = head_ref[k], offset_ref[k]
            net = jnp.where(row >= o, pltpu.roll(net, o, 1), pltpu.roll(prev_ref[k], o, 1))
        nets.append((net[:, :, :cols], pltpu.roll(net, WINDOW - cols, 2)[:, :, :cols]))
    count = planes // 2
    for part in range(2):
        span = slice(part * count, (part + 1) * count)
        held = state_ref[0, 0, span]
        answer = fit_ref[0, span]
        joined = share[0] * (2.0 * answer - held)
        for k in range(3):
            joined = joined + share[k + 1] * (state_ref[k + 1, 0, span] - 2.0 * nets[k][part])
        next_ref[0, 0, span] = held + joined - answer
        for k in range(3):
            next_ref[k + 1, 0, span] = joined + nets[k][part]


VMEM = pl.BlockSpec(memory_space=pltpu.VMEM)
PARAMS = pltpu.CompilerParams(vmem_limit_bytes=20 * 1024 * 1024)
HBM = pl.BlockSpec(memory_space=pltpu.HBM)
SMEM = pl.BlockSpec(memory_space=pltpu.SMEM)


def cost(micros):
    return pl.CostEstimate(flops=micros * 10**9, bytes_accessed=micros * 3 * 10**6, transcendentals=0)


def hop(value, axis, step):
    count = lax.axis_size(axis)
    return lax.ppermute(value, axis, [(i, (i + step) % count) for i in range(count)])


def step(
    agent_state, measured, bin_index, bin_frac, patch_offsets, agent_weights, up_weight, down_weight
):
    planes, row_count, col_count = agent_state.shape[2:]
    tile_count = lax.axis_size("tile")
    agent_count = lax.axis_size("agent")
    angles = bin_index.shape[0]
    pixels = row_count * col_count
    factor = 1.0 / math.sqrt(angles * (row_count * tile_count + col_count * agent_count))
    both = ("tile", "agent")
    f32 = jnp.float32

    shape = (planes // 2, row_count, 2 * col_count)
    coded = (planes // 2 + 1, row_count, 2 * col_count)
    head, tail, volume, bins, nums = pl.pallas_call(
        pack_kernel,
        out_shape=[
            jax.ShapeDtypeStruct((2,) + shape, jnp.bfloat16),
            jax.ShapeDtypeStruct((1,) + shape, jnp.bfloat16),
            jax.ShapeDtypeStruct(agent_state.shape[2:], f32),
            jax.ShapeDtypeStruct(bin_index.shape, jnp.int32),
            jax.ShapeDtypeStruct(bin_frac.shape, jnp.int32),
        ],
        in_specs=[HBM] * 3,
        out_specs=[VMEM] * 5,
        scratch_shapes=[
            pltpu.VMEM((3,) + agent_state.shape[2:], f32),
            pltpu.SemaphoreType.DMA((4,)),
        ],
        compiler_params=pltpu.CompilerParams(vmem_limit_bytes=56000000),
        cost_estimate=cost(2),
        name="pack",
    )(agent_state, bin_index, bin_frac)
    following = hop(head, "tile", -1)

    group = (lax.axis_index("tile") * agent_count // planes).astype(jnp.int32)
    pieces, flat, rel, near = pl.pallas_call(
        project_kernel,
        out_shape=[
            jax.ShapeDtypeStruct((2 * angles * planes, WINDOW), f32),
            jax.ShapeDtypeStruct((planes, pixels), f32),
            jax.ShapeDtypeStruct((angles, pixels), jnp.int32),
            jax.ShapeDtypeStruct((angles, pixels), f32),
        ],
        in_specs=[SMEM] + [VMEM] * 4,
        out_specs=[VMEM] * 4,
        scratch_shapes=[pltpu.VMEM((angles, WINDOW), f32)],
        compiler_params=PARAMS,
        cost_estimate=cost(5),
        name="project",
    )(group.reshape(1), volume, bins, nums, measured)

    region = pl.pallas_call(
        shift_kernel,
        out_shape=jax.ShapeDtypeStruct((3,) + shape, jnp.bfloat16),
        in_specs=[SMEM, VMEM, VMEM, VMEM],
        out_specs=VMEM,
        compiler_params=PARAMS,
        cost_estimate=cost(1),
        name="shift",
    )(patch_offsets, head, tail, following)
    others = []
    for step in range(1, agent_count):
        others.append(hop(region, "agent", -step))

    count = angles * planes
    got = lax.all_to_all(pieces.reshape(count, 2, WINDOW), both, 0, 0, tiled=True)
    cut = pl.pallas_call(
        functools.partial(combine_kernel, factor, measured.shape[2]),
        out_shape=jax.ShapeDtypeStruct((angles * planes, WINDOW), f32),
        in_specs=[VMEM],
        out_specs=VMEM,
        compiler_params=PARAMS,
        cost_estimate=cost(2),
        name="combine",
    )(got.reshape(2 * count, WINDOW))

    back = lax.all_to_all(cut, both, 0, 0, tiled=True)
    own, far = pl.pallas_call(
        denoise_kernel,
        out_shape=[
            jax.ShapeDtypeStruct((2, 3) + shape, f32),
            jax.ShapeDtypeStruct((2, 3) + coded, WIRE),
        ],
        in_specs=[SMEM] + [VMEM] * 4 + [HBM] * 2,
        out_specs=[VMEM] * 2,
        scratch_shapes=[
            pltpu.VMEM(up_weight.shape, up_weight.dtype),
            pltpu.VMEM(down_weight.shape, down_weight.dtype),
            pltpu.SemaphoreType.DMA((6,)),
        ],
        compiler_params=pltpu.CompilerParams(vmem_limit_bytes=54500000),
        cost_estimate=cost(6),
        name="denoise",
    )(patch_offsets, region, *others, up_weight, down_weight)
    opposite = hop(far, "agent", 2)
    kept, passed = pl.pallas_call(
        halve_kernel,
        out_shape=[
            jax.ShapeDtypeStruct((3,) + shape, f32),
            jax.ShapeDtypeStruct((3,) + coded, WIRE),
        ],
        in_specs=[VMEM] * 2,
        out_specs=[VMEM] * 2,
        compiler_params=PARAMS,
        cost_estimate=cost(1),
        name="halve",
    )(own, opposite)
    beside = hop(passed, "agent", 1)

    fit, held = pl.pallas_call(
        functools.partial(spread_kernel, factor),
        out_shape=[jax.ShapeDtypeStruct(agent_state.shape[1:], f32)] * 2,
        in_specs=[VMEM] * 4,
        out_specs=[VMEM] * 2,
        compiler_params=PARAMS,
        cost_estimate=cost(4),
        name="spread",
    )(flat, rel, near, back.reshape(angles, planes, WINDOW))
    head, tail = pl.pallas_call(
        add_kernel,
        out_shape=[
            jax.ShapeDtypeStruct((2,) + shape, f32),
            jax.ShapeDtypeStruct((1,) + shape, f32),
        ],
        in_specs=[VMEM] * 2,
        out_specs=[VMEM] * 2,
        compiler_params=PARAMS,
        cost_estimate=cost(1),
        name="add",
    )(kept, beside)
    previous = hop(head, "tile", 1)
    state_next = pl.pallas_call(
        join_kernel,
        out_shape=jax.ShapeDtypeStruct(agent_state.shape, f32),
        in_specs=[SMEM, SMEM] + [VMEM] * 5,
        out_specs=VMEM,
        compiler_params=PARAMS,
        cost_estimate=cost(2),
        name="join",
    )(patch_offsets, agent_weights, agent_state, held, head, tail, previous)
    return (state_next, fit)


def solution(mesh):
    placed = (
        P(None, None, None, "tile", "agent"),
        P(None, None, ("tile", "agent")),
        P(None, "tile", "agent"),
        P(None, "tile", "agent"),
        P(),
        P(),
        P(None, None, "agent"),
        P(None, "agent", None),
    )
    return jax.shard_map(
        step,
        mesh=mesh,
        in_specs=placed,
        out_specs=(P(None, None, None, "tile", "agent"), P(None, None, "tile", "agent")),
        check_vma=False,
    )
```

```python
import functools
import math

import jax
import jax.numpy as jnp
from jax import lax
from jax.experimental import pallas as pl
from jax.experimental.pallas import tpu as pltpu
from jax.sharding import PartitionSpec as P


PATCH = 16
SCALE = 724
WINDOW = 128
ALIGN = 32
WIRE = jnp.int16
STEPS = 32700.0
GRAIN = 128.0


def split_two(value):
    high = value.astype(jnp.bfloat16)
    return high, (value - high.astype(jnp.float32)).astype(jnp.bfloat16)


def window_starts(low):
    return (jnp.min(low, axis=1, keepdims=True) // ALIGN) * ALIGN


def one_hot(rel_row):
    spots = lax.broadcasted_iota(jnp.int32, (WINDOW, rel_row.shape[1]), 0)
    return jnp.where(spots == rel_row, 1.0, 0.0).astype(jnp.bfloat16)


def project_kernel(
    group_ref, state_ref, bin_ref, num_ref, meas_ref, out_ref, u_ref, rel_ref, w_ref, start_ref
):
    out_ref[...] = jnp.zeros_like(out_ref)
    angles, rows, cols = bin_ref.shape
    planes = state_ref.shape[0]
    for x in range(rows):
        span = slice(x * cols, (x + 1) * cols)
        u_ref[:, span] = state_ref[:, x, :]
        rel_ref[:, span] = bin_ref[:, x, :]
        w_ref[:, span] = num_ref[:, x, :].astype(jnp.float32) * (1.0 / SCALE)
    low = rel_ref[...]
    start = window_starts(low)
    rel_ref[...] = low - start
    start_ref[...] = jnp.broadcast_to(start.astype(jnp.float32), (angles, WINDOW))
    owned = meas_ref.shape[2]
    mine = pl.multiple_of(group_ref[0] * (2 * planes), 2 * planes)
    out_ref[pl.ds(mine + 1, planes, stride=2), :owned] = meas_ref[0]
    lane = lax.broadcasted_iota(jnp.int32, (planes, WINDOW), 1)

    def body(a, carry):
        band = one_hot(rel_ref[pl.ds(a, 1), :])
        u = u_ref[...]
        near = u * w_ref[pl.ds(a, 1), :]
        near_hi, near_lo = split_two(near)
        far_hi, far_lo = split_two(u - near)
        terms = jnp.concatenate([near_hi, near_lo, far_hi, far_lo], axis=0)
        sums = lax.dot_general(
            terms, band, (((1,), (1,)), ((), ())), preferred_element_type=jnp.float32
        )
        at_low = sums[:planes] + sums[planes : 2 * planes]
        above = sums[2 * planes : 3 * planes] + sums[3 * planes :]
        piece = at_low + pltpu.roll(above, 1, 1)
        piece = jnp.where(lane == WINDOW - 1, start_ref[pl.ds(a, 1), :], piece)
        first = pl.multiple_of(a * (2 * planes), 2 * planes)
        out_ref[pl.ds(first, planes, stride=2), :] = piece
        return carry

    lax.fori_loop(0, angles, body, 0, unroll=16)


def combine_kernel(factor, owned, got_ref, out_ref):
    count = got_ref.shape[0] // 2
    step = WINDOW // ALIGN
    rows = 16
    got = got_ref[pl.ds(0, count, stride=2), :]
    lane_all = lax.broadcasted_iota(jnp.int32, (count, WINDOW), 1)
    piece = jnp.where(lane_all < WINDOW - 1, got, 0.0)
    block = got[:, WINDOW - 1 :].astype(jnp.int32) // ALIGN
    slot = (block % step) * rows + block // step
    slots = lax.broadcasted_iota(jnp.int32, (count, step * rows), 1)
    route = jnp.where(slots == slot, 1.0, 0.0).astype(jnp.bfloat16)
    sums = lax.dot_general(
        route,
        jnp.concatenate(split_two(piece), axis=1),
        (((0,), (0,)), ((), ())),
        preferred_element_type=jnp.float32,
    )
    sums = sums[:, :WINDOW] + sums[:, WINDOW:]
    lane = lax.broadcasted_iota(jnp.int32, (rows, WINDOW), 1)
    row = lax.broadcasted_iota(jnp.int32, (rows, WINDOW), 0)
    sino = sums[:rows]
    for m in range(1, step):
        turned = pltpu.roll(sums[m * rows : (m + 1) * rows], m * ALIGN, 1)
        here = lane >= m * ALIGN
        sino = sino + jnp.where(here, turned, 0.0)
        sino = sino + pltpu.roll(jnp.where(here, 0.0, turned), 1, 0)
    sent = got_ref[pl.ds(1, count, stride=2), :]
    taken = jnp.sum(sent.reshape(count // 16, 16, WINDOW), axis=0)
    taken = jnp.where(lax.broadcasted_iota(jnp.int32, taken.shape, 1) < owned, taken, 0.0)
    target = jnp.zeros_like(sino)
    for i in range(16):
        first, off = divmod(i * owned, WINDOW)
        turned = taken[i : i + 1]
        if off:
            turned = pltpu.roll(turned, off, 1)
        hit = ((row == first) & (lane >= off)) | ((row == first + 1) & (lane < off))
        target = target + jnp.where(hit, turned, 0.0)
    misfit = factor * sino - target
    views = [misfit]
    for m in range(1, step):
        turned = pltpu.roll(misfit, WINDOW - m * ALIGN, 1)
        views.append(
            jnp.where(lane < WINDOW - m * ALIGN, turned, pltpu.roll(turned, rows - 1, 0))
        )
    views = jnp.concatenate(views, axis=0)
    cut = jnp.dot(
        route, jnp.concatenate(split_two(views), axis=1), preferred_element_type=jnp.float32
    )
    out_ref[...] = cut[:, :WINDOW] + cut[:, WINDOW:]


def pack_kernel(
    state_hbm, bin_hbm, num_hbm, head_ref, tail_ref, first_ref, bin_ref, num_ref, state_ref, sems
):
    load = pltpu.make_async_copy(state_hbm.at[pl.ds(1, 3), 0], state_ref, sems.at[0])
    ahead = [
        pltpu.make_async_copy(state_hbm.at[0, 0], first_ref, sems.at[1]),
        pltpu.make_async_copy(bin_hbm, bin_ref, sems.at[2]),
        pltpu.make_async_copy(num_hbm, num_ref, sems.at[3]),
    ]
    for copy in [load] + ahead:
        copy.start()
    load.wait()
    half, cols = state_ref.shape[1] // 2, state_ref.shape[3]
    for k in range(3):
        out = head_ref.at[k] if k < 2 else tail_ref.at[0]
        for part in range(2):
            block = state_ref[k, part * half : (part + 1) * half]
            out[:, :, part * cols : (part + 1) * cols] = block.astype(out.dtype)
    for copy in ahead:
        copy.wait()


def shift_kernel(offset_ref, head_ref, tail_ref, next_ref, out_ref):
    rows = head_ref.shape[2]
    for k in range(2):
        o = offset_ref[k]
        own = pltpu.roll(head_ref[k].astype(jnp.float32), rows - o, 1)
        more = pltpu.roll(next_ref[k].astype(jnp.float32), rows - o, 1)
        row = lax.broadcasted_iota(jnp.int32, own.shape, 1)
        out_ref[k] = jnp.where(row < rows - o, own, more).astype(out_ref.dtype)
    out_ref[2] = tail_ref[0]


def encode(block, out):
    count = block.shape[0]
    top = jnp.max(jnp.max(jnp.abs(block), axis=0), axis=0, keepdims=True)
    level = jnp.ceil(jnp.log2(jnp.maximum(top, 1e-30)) * GRAIN)
    scale = STEPS * jnp.exp2(level * (-1.0 / GRAIN))
    out[:count] = jnp.round(block * scale[None]).astype(jnp.int32).astype(out.dtype)
    level = jnp.broadcast_to(level, block.shape[1:])
    out[count] = level.astype(jnp.int32).astype(out.dtype)


def decode(held):
    count = held.shape[0] - 1
    level = held[count].astype(jnp.float32)[:1]
    scale = (1.0 / STEPS) * jnp.exp2(level * (1.0 / GRAIN))
    return held[:count].astype(jnp.float32) * scale[None]


def halve_kernel(near_ref, got_ref, head_ref, tail_ref, send_ref, ahead_ref):
    for k in range(3):
        out = head_ref.at[k] if k < 2 else tail_ref.at[0]
        out[...] = near_ref[0, k] + decode(got_ref.at[0, k])
        encode(near_ref[1, k] + decode(got_ref.at[1, k]), send_ref.at[k])
    ahead_ref[...] = send_ref[:2]


def swap_slabs(slabs):
    lane = lax.broadcasted_iota(jnp.int32, slabs[0].shape, 1)
    width = slabs[0].shape[1]
    slabs = list(slabs)
    for step in (1, 2, 4, 8):
        odd = (lane & step) != 0
        for i in range(len(slabs)):
            if i & step:
                continue
            first, second = slabs[i], slabs[i + step]
            slabs[i] = jnp.where(odd, pltpu.roll(second, step, 1), first)
            slabs[i + step] = jnp.where(odd, second, pltpu.roll(first, width - step, 1))
    return slabs


def swap_rows(slab):
    width = slab.shape[1]
    top, low = slab[:8], slab[8:]
    lane = lax.broadcasted_iota(jnp.int32, top.shape, 1)
    row = lax.broadcasted_iota(jnp.int32, top.shape, 0)
    odd = (lane & 8) != 0
    top, low = (
        jnp.where(odd, pltpu.roll(low, 8, 1), top),
        jnp.where(odd, low, pltpu.roll(top, width - 8, 1)),
    )
    halves = []
    for half in (top, low):
        for step in (1, 2, 4):
            odd_lane, odd_row = (lane & step) != 0, (row & step) != 0
            up = pltpu.roll(pltpu.roll(half, 8 - step, 0), step, 1)
            down = pltpu.roll(pltpu.roll(half, step, 0), width - step, 1)
            other = jnp.where(odd_lane, up, down)
            half = jnp.where(odd_lane == odd_row, half, other)
        halves.append(half)
    return jnp.concatenate(halves, axis=0)


def denoise_kernel(
    offset_ref, p0, p1, p2, p3, up_hbm, down_hbm, near_ref, far_ref, up_ref, down_ref, sems
):
    loads = []
    for k in range(3):
        up = pltpu.make_async_copy(up_hbm.at[k], up_ref.at[k], sems.at[k])
        down = pltpu.make_async_copy(down_hbm.at[k], down_ref.at[k], sems.at[3 + k])
        up.start()
        down.start()
        loads.append((up, down))
    side = PATCH
    size = side * side
    row = lax.broadcasted_iota(jnp.int32, (size, size), 0)
    col = lax.broadcasted_iota(jnp.int32, (size, size), 1)
    turned = (row % side) * side + row // side
    exchange = jnp.where(col == turned, 1.0, 0.0).astype(jnp.bfloat16)
    lane = lax.broadcasted_iota(jnp.int32, (size // 2, WINDOW), 1)
    left = lane < WINDOW // 2
    wide = lax.broadcasted_iota(jnp.int32, (size, WINDOW), 1)

    def joined(a, b):
        a = a.reshape(size // 2, WINDOW).astype(jnp.float32)
        b = b.reshape(size // 2, WINDOW).astype(jnp.float32)
        early = jnp.where(left, a, pltpu.roll(b, WINDOW // 2, 1))
        late = jnp.where(left, pltpu.roll(a, WINDOW // 2, 1), b)
        return jnp.concatenate([early, late], axis=0)

    def slabs_of(half):
        return [half[i * side : (i + 1) * side] for i in range(side)]

    def arrange(which, half):
        if which == 0:
            return jnp.concatenate(swap_slabs(slabs_of(half)), axis=0)
        if which == 2:
            return jnp.concatenate([swap_rows(slab) for slab in slabs_of(half)], axis=0)
        return half

    for k in range(3):
        halves = [joined(p0[k], p1[k]), joined(p2[k], p3[k])]
        if k != 1:
            o = offset_ref[k]
            a, b = [pltpu.roll(half, WINDOW - o, 1) for half in halves]
            inside = wide < WINDOW - o
            halves = [jnp.where(inside, a, b), jnp.where(inside, b, a)]
        halves = [arrange(k, half) for half in halves]
        patches = jnp.concatenate([half.T for half in halves], axis=0).astype(jnp.bfloat16)
        for load in loads[k]:
            load.wait()
        down = down_ref[k]
        if k == 0:
            patches = jnp.dot(
                patches, exchange, preferred_element_type=jnp.float32
            ).astype(jnp.bfloat16)
            down = jnp.dot(down, exchange, preferred_element_type=jnp.float32).astype(jnp.bfloat16)
        hidden = jnp.dot(patches, up_ref[k], preferred_element_type=jnp.float32)
        hidden = jnp.maximum(hidden, 0.0).astype(jnp.bfloat16)
        result = jnp.dot(hidden, down, preferred_element_type=jnp.float32)
        halves = [arrange(k, result[:WINDOW].T), arrange(k, result[WINDOW:].T)]
        if k != 1:
            a, b = [pltpu.roll(half, o, 1) for half in halves]
            inside = wide >= o
            halves = [jnp.where(inside, a, b), jnp.where(inside, b, a)]
        for half, near in ((halves[0], True), (halves[1], False)):
            early, late = half[: size // 2], half[size // 2 :]
            blocks = (
                jnp.where(left, early, pltpu.roll(late, WINDOW // 2, 1)),
                jnp.where(left, pltpu.roll(early, WINDOW // 2, 1), late),
            )
            for j in range(2):
                block = blocks[j].reshape(near_ref.shape[2:])
                if near:
                    near_ref[j, k] = block
                else:
                    encode(block, far_ref.at[j, k])


def spread_kernel(factor, u_ref, rel_ref, w_ref, win_ref, fit_ref, copy_ref):
    angles, planes, _ = win_ref.shape

    def body(a, total):
        band = one_hot(rel_ref[pl.ds(a, 1), :])
        at_low = win_ref[a]
        above = pltpu.roll(at_low, WINDOW - 1, 1)
        terms = jnp.concatenate(split_two(at_low) + split_two(above), axis=0)
        picked = jnp.dot(terms, band, preferred_element_type=jnp.float32)
        near = picked[:planes] + picked[planes : 2 * planes]
        far = picked[2 * planes : 3 * planes] + picked[3 * planes :]
        w = w_ref[pl.ds(a, 1), :]
        return total + (far + w * (near - far))

    total = lax.fori_loop(0, angles, body, jnp.zeros(u_ref.shape, jnp.float32), unroll=16)
    fit = u_ref[...] - factor * total
    rows, cols = fit_ref.shape[2:]
    for x in range(rows):
        fit_ref[0, :, x, :] = fit[:, x * cols : (x + 1) * cols]
    copy_ref[...] = fit_ref[...]


def join_kernel(
    offset_ref, weight_ref, state_ref, fit_ref, head_ref, tail_ref, beside_ref, prev_ref, side_ref,
    next_ref,
):
    planes, _, cols = fit_ref.shape[1:]
    raw = [jnp.full((1, cols), weight_ref[i], jnp.float32) for i in range(4)]
    whole = raw[0] + raw[1] + raw[2] + raw[3]
    share = [value / whole for value in raw]
    row = lax.broadcasted_iota(jnp.int32, tail_ref.shape[1:], 1)
    nets = []
    for k in range(3):
        if k == 2:
            net = tail_ref[0] + decode(beside_ref.at[k])
        else:
            o = offset_ref[k]
            net = head_ref[k] + decode(beside_ref.at[k])
            before = prev_ref[k] + decode(side_ref.at[k])
            net = jnp.where(row >= o, pltpu.roll(net, o, 1), pltpu.roll(before, o, 1))
        nets.append((net[:, :, :cols], pltpu.roll(net, WINDOW - cols, 2)[:, :, :cols]))
    count = planes // 2
    for part in range(2):
        span = slice(part * count, (part + 1) * count)
        held = state_ref[0, 0, span]
        answer = fit_ref[0, span]
        joined = share[0] * (2.0 * answer - held)
        for k in range(3):
            joined = joined + share[k + 1] * (state_ref[k + 1, 0, span] - 2.0 * nets[k][part])
        next_ref[0, 0, span] = held + joined - answer
        for k in range(3):
            next_ref[k + 1, 0, span] = joined + nets[k][part]


VMEM = pl.BlockSpec(memory_space=pltpu.VMEM)
PARAMS = pltpu.CompilerParams(vmem_limit_bytes=20 * 1024 * 1024)
HBM = pl.BlockSpec(memory_space=pltpu.HBM)
SMEM = pl.BlockSpec(memory_space=pltpu.SMEM)


def cost(micros):
    return pl.CostEstimate(flops=micros * 10**9, bytes_accessed=micros * 3 * 10**6, transcendentals=0)


def hop(value, axis, step):
    count = lax.axis_size(axis)
    return lax.ppermute(value, axis, [(i, (i + step) % count) for i in range(count)])


def step(
    agent_state, measured, bin_index, bin_frac, patch_offsets, agent_weights, up_weight, down_weight
):
    planes, row_count, col_count = agent_state.shape[2:]
    tile_count = lax.axis_size("tile")
    agent_count = lax.axis_size("agent")
    angles = bin_index.shape[0]
    pixels = row_count * col_count
    factor = 1.0 / math.sqrt(angles * (row_count * tile_count + col_count * agent_count))
    both = ("tile", "agent")
    f32 = jnp.float32

    shape = (planes // 2, row_count, 2 * col_count)
    coded = (planes // 2 + 1, row_count, 2 * col_count)
    head, tail, volume, bins, nums = pl.pallas_call(
        pack_kernel,
        out_shape=[
            jax.ShapeDtypeStruct((2,) + shape, jnp.bfloat16),
            jax.ShapeDtypeStruct((1,) + shape, jnp.bfloat16),
            jax.ShapeDtypeStruct(agent_state.shape[2:], f32),
            jax.ShapeDtypeStruct(bin_index.shape, jnp.int32),
            jax.ShapeDtypeStruct(bin_frac.shape, jnp.int32),
        ],
        in_specs=[HBM] * 3,
        out_specs=[VMEM] * 5,
        scratch_shapes=[
            pltpu.VMEM((3,) + agent_state.shape[2:], f32),
            pltpu.SemaphoreType.DMA((4,)),
        ],
        compiler_params=pltpu.CompilerParams(vmem_limit_bytes=56000000),
        cost_estimate=cost(2),
        name="pack",
    )(agent_state, bin_index, bin_frac)
    following = hop(head, "tile", -1)

    group = (lax.axis_index("tile") * agent_count // planes).astype(jnp.int32)
    pieces, flat, rel, near = pl.pallas_call(
        project_kernel,
        out_shape=[
            jax.ShapeDtypeStruct((2 * angles * planes, WINDOW), f32),
            jax.ShapeDtypeStruct((planes, pixels), f32),
            jax.ShapeDtypeStruct((angles, pixels), jnp.int32),
            jax.ShapeDtypeStruct((angles, pixels), f32),
        ],
        in_specs=[SMEM] + [VMEM] * 4,
        out_specs=[VMEM] * 4,
        scratch_shapes=[pltpu.VMEM((angles, WINDOW), f32)],
        compiler_params=PARAMS,
        cost_estimate=cost(5),
        name="project",
    )(group.reshape(1), volume, bins, nums, measured)

    region = pl.pallas_call(
        shift_kernel,
        out_shape=jax.ShapeDtypeStruct((3,) + shape, jnp.bfloat16),
        in_specs=[SMEM, VMEM, VMEM, VMEM],
        out_specs=VMEM,
        compiler_params=PARAMS,
        cost_estimate=cost(1),
        name="shift",
    )(patch_offsets, head, tail, following)
    others = []
    for step in range(1, agent_count):
        others.append(hop(region, "agent", -step))

    count = angles * planes
    got = lax.all_to_all(pieces.reshape(count, 2, WINDOW), both, 0, 0, tiled=True)
    cut = pl.pallas_call(
        functools.partial(combine_kernel, factor, measured.shape[2]),
        out_shape=jax.ShapeDtypeStruct((angles * planes, WINDOW), f32),
        in_specs=[VMEM],
        out_specs=VMEM,
        compiler_params=PARAMS,
        cost_estimate=cost(2),
        name="combine",
    )(got.reshape(2 * count, WINDOW))

    back = lax.all_to_all(cut, both, 0, 0, tiled=True)
    own, far = pl.pallas_call(
        denoise_kernel,
        out_shape=[
            jax.ShapeDtypeStruct((2, 3) + shape, f32),
            jax.ShapeDtypeStruct((2, 3) + coded, WIRE),
        ],
        in_specs=[SMEM] + [VMEM] * 4 + [HBM] * 2,
        out_specs=[VMEM] * 2,
        scratch_shapes=[
            pltpu.VMEM(up_weight.shape, up_weight.dtype),
            pltpu.VMEM(down_weight.shape, down_weight.dtype),
            pltpu.SemaphoreType.DMA((6,)),
        ],
        compiler_params=pltpu.CompilerParams(vmem_limit_bytes=54500000),
        cost_estimate=cost(6),
        name="denoise",
    )(patch_offsets, region, *others, up_weight, down_weight)
    opposite = hop(far, "agent", 2)
    head, tail, passed, ahead = pl.pallas_call(
        halve_kernel,
        out_shape=[
            jax.ShapeDtypeStruct((2,) + shape, f32),
            jax.ShapeDtypeStruct((1,) + shape, f32),
            jax.ShapeDtypeStruct((3,) + coded, WIRE),
            jax.ShapeDtypeStruct((2,) + coded, WIRE),
        ],
        in_specs=[VMEM] * 2,
        out_specs=[VMEM] * 4,
        compiler_params=PARAMS,
        cost_estimate=cost(1),
        name="halve",
    )(own, opposite)
    beside = hop(passed, "agent", 1)
    pairs = [
        (t * agent_count + g, (t + 1) % tile_count * agent_count + (g + 1) % agent_count)
        for t in range(tile_count)
        for g in range(agent_count)
    ]
    side = lax.ppermute(ahead, both, pairs)
    previous = hop(head, "tile", 1)

    fit, held = pl.pallas_call(
        functools.partial(spread_kernel, factor),
        out_shape=[jax.ShapeDtypeStruct(agent_state.shape[1:], f32)] * 2,
        in_specs=[VMEM] * 4,
        out_specs=[VMEM] * 2,
        compiler_params=PARAMS,
        cost_estimate=cost(4),
        name="spread",
    )(flat, rel, near, back.reshape(angles, planes, WINDOW))
    state_next = pl.pallas_call(
        join_kernel,
        out_shape=jax.ShapeDtypeStruct(agent_state.shape, f32),
        in_specs=[SMEM, SMEM] + [VMEM] * 7,
        out_specs=VMEM,
        compiler_params=PARAMS,
        cost_estimate=cost(2),
        name="join",
    )(patch_offsets, agent_weights, agent_state, held, head, tail, beside, previous, side)
    return (state_next, fit)


def solution(mesh):
    placed = (
        P(None, None, None, "tile", "agent"),
        P(None, None, ("tile", "agent")),
        P(None, "tile", "agent"),
        P(None, "tile", "agent"),
        P(),
        P(),
        P(None, None, "agent"),
        P(None, "agent", None),
    )
    return jax.shard_map(
        step,
        mesh=mesh,
        in_specs=placed,
        out_specs=(P(None, None, None, "tile", "agent"), P(None, None, "tile", "agent")),
        check_vma=False,
    )
```

```python
import functools
import math

import jax
import jax.numpy as jnp
from jax import lax
from jax.experimental import pallas as pl
from jax.experimental.pallas import tpu as pltpu
from jax.sharding import PartitionSpec as P


PATCH = 16
SCALE = 724
WINDOW = 128
ALIGN = 32
WIRE = jnp.int16
STEPS = 32700.0
GRAIN = 128.0


def split_two(value):
    high = value.astype(jnp.bfloat16)
    return high, (value - high.astype(jnp.float32)).astype(jnp.bfloat16)


def window_starts(low):
    return (jnp.min(low, axis=1, keepdims=True) // ALIGN) * ALIGN


def one_hot(rel_row):
    spots = lax.broadcasted_iota(jnp.int32, (WINDOW, rel_row.shape[1]), 0)
    return jnp.where(spots == rel_row, 1.0, 0.0).astype(jnp.bfloat16)


def project_kernel(
    group_ref, state_ref, bin_ref, num_ref, meas_ref, out_ref, u_ref, rel_ref, w_ref, start_ref
):
    out_ref[...] = jnp.zeros_like(out_ref)
    angles, rows, cols = bin_ref.shape
    planes = state_ref.shape[0]
    for x in range(rows):
        span = slice(x * cols, (x + 1) * cols)
        u_ref[:, span] = state_ref[:, x, :]
        rel_ref[:, span] = bin_ref[:, x, :]
        w_ref[:, span] = num_ref[:, x, :].astype(jnp.float32) * (1.0 / SCALE)
    low = rel_ref[...]
    start = window_starts(low)
    rel_ref[...] = low - start
    start_ref[...] = jnp.broadcast_to(start.astype(jnp.float32), (angles, WINDOW))
    owned = meas_ref.shape[2]
    mine = pl.multiple_of(group_ref[0] * (2 * planes), 2 * planes)
    out_ref[pl.ds(mine + 1, planes, stride=2), :owned] = meas_ref[0]
    lane = lax.broadcasted_iota(jnp.int32, (planes, WINDOW), 1)

    def body(a, carry):
        band = one_hot(rel_ref[pl.ds(a, 1), :])
        u = u_ref[...]
        near = u * w_ref[pl.ds(a, 1), :]
        near_hi, near_lo = split_two(near)
        far_hi, far_lo = split_two(u - near)
        terms = jnp.concatenate([near_hi, near_lo, far_hi, far_lo], axis=0)
        sums = lax.dot_general(
            terms, band, (((1,), (1,)), ((), ())), preferred_element_type=jnp.float32
        )
        at_low = sums[:planes] + sums[planes : 2 * planes]
        above = sums[2 * planes : 3 * planes] + sums[3 * planes :]
        piece = at_low + pltpu.roll(above, 1, 1)
        piece = jnp.where(lane == WINDOW - 1, start_ref[pl.ds(a, 1), :], piece)
        first = pl.multiple_of(a * (2 * planes), 2 * planes)
        out_ref[pl.ds(first, planes, stride=2), :] = piece
        return carry

    lax.fori_loop(0, angles, body, 0, unroll=16)


def combine_kernel(factor, owned, got_ref, out_ref):
    count = got_ref.shape[0] // 2
    step = WINDOW // ALIGN
    rows = 16
    got = got_ref[pl.ds(0, count, stride=2), :]
    lane_all = lax.broadcasted_iota(jnp.int32, (count, WINDOW), 1)
    piece = jnp.where(lane_all < WINDOW - 1, got, 0.0)
    block = got[:, WINDOW - 1 :].astype(jnp.int32) // ALIGN
    slot = (block % step) * rows + block // step
    slots = lax.broadcasted_iota(jnp.int32, (count, step * rows), 1)
    route = jnp.where(slots == slot, 1.0, 0.0).astype(jnp.bfloat16)
    sums = lax.dot_general(
        route,
        jnp.concatenate(split_two(piece), axis=1),
        (((0,), (0,)), ((), ())),
        preferred_element_type=jnp.float32,
    )
    sums = sums[:, :WINDOW] + sums[:, WINDOW:]
    lane = lax.broadcasted_iota(jnp.int32, (rows, WINDOW), 1)
    row = lax.broadcasted_iota(jnp.int32, (rows, WINDOW), 0)
    sino = sums[:rows]
    for m in range(1, step):
        turned = pltpu.roll(sums[m * rows : (m + 1) * rows], m * ALIGN, 1)
        here = lane >= m * ALIGN
        sino = sino + jnp.where(here, turned, 0.0)
        sino = sino + pltpu.roll(jnp.where(here, 0.0, turned), 1, 0)
    sent = got_ref[pl.ds(1, count, stride=2), :]
    taken = jnp.sum(sent.reshape(count // 16, 16, WINDOW), axis=0)
    taken = jnp.where(lax.broadcasted_iota(jnp.int32, taken.shape, 1) < owned, taken, 0.0)
    target = jnp.zeros_like(sino)
    for i in range(16):
        first, off = divmod(i * owned, WINDOW)
        turned = taken[i : i + 1]
        if off:
            turned = pltpu.roll(turned, off, 1)
        hit = ((row == first) & (lane >= off)) | ((row == first + 1) & (lane < off))
        target = target + jnp.where(hit, turned, 0.0)
    misfit = factor * sino - target
    views = [misfit]
    for m in range(1, step):
        turned = pltpu.roll(misfit, WINDOW - m * ALIGN, 1)
        views.append(
            jnp.where(lane < WINDOW - m * ALIGN, turned, pltpu.roll(turned, rows - 1, 0))
        )
    views = jnp.concatenate(views, axis=0)
    cut = jnp.dot(
        route, jnp.concatenate(split_two(views), axis=1), preferred_element_type=jnp.float32
    )
    out_ref[...] = cut[:, :WINDOW] + cut[:, WINDOW:]


def pack_kernel(
    state_hbm, bin_hbm, num_hbm, head_ref, tail_ref, first_ref, bin_ref, num_ref, state_ref, sems
):
    load = pltpu.make_async_copy(state_hbm.at[pl.ds(1, 3), 0], state_ref, sems.at[0])
    ahead = [
        pltpu.make_async_copy(state_hbm.at[0, 0], first_ref, sems.at[1]),
        pltpu.make_async_copy(bin_hbm, bin_ref, sems.at[2]),
        pltpu.make_async_copy(num_hbm, num_ref, sems.at[3]),
    ]
    for copy in [load] + ahead:
        copy.start()
    load.wait()
    half, cols = state_ref.shape[1] // 2, state_ref.shape[3]
    for k in range(3):
        out = head_ref.at[k] if k < 2 else tail_ref.at[0]
        for part in range(2):
            block = state_ref[k, part * half : (part + 1) * half]
            out[:, :, part * cols : (part + 1) * cols] = block.astype(out.dtype)
    for copy in ahead:
        copy.wait()


def shift_kernel(offset_ref, head_ref, tail_ref, next_ref, out_ref):
    rows = head_ref.shape[2]
    for k in range(2):
        o = offset_ref[k]
        own = pltpu.roll(head_ref[k].astype(jnp.float32), rows - o, 1)
        more = pltpu.roll(next_ref[k].astype(jnp.float32), rows - o, 1)
        row = lax.broadcasted_iota(jnp.int32, own.shape, 1)
        out_ref[k] = jnp.where(row < rows - o, own, more).astype(out_ref.dtype)
    out_ref[2] = tail_ref[0]


def encode(block, out):
    count = block.shape[0]
    top = jnp.max(jnp.max(jnp.abs(block), axis=0), axis=0, keepdims=True)
    level = jnp.ceil(jnp.log2(jnp.maximum(top, 1e-30)) * GRAIN)
    scale = STEPS * jnp.exp2(level * (-1.0 / GRAIN))
    rows = count * block.shape[1]
    steps = jnp.round(block * scale[None]).reshape(rows, block.shape[2])
    out[:rows] = steps.astype(jnp.int32).astype(out.dtype)
    level = jnp.broadcast_to(level, (8, block.shape[2]))
    out[rows:] = level.astype(jnp.int32).astype(out.dtype)


def decode(held):
    rows = held.shape[0] - 8
    level = held[rows:].astype(jnp.float32)[:1]
    scale = (1.0 / STEPS) * jnp.exp2(level * (1.0 / GRAIN))
    steps = held[:rows].astype(jnp.float32) * scale
    return steps.reshape(rows // PATCH, PATCH, steps.shape[1])


def halve_kernel(near_ref, got_ref, head_ref, tail_ref, send_ref, ahead_ref):
    for k in range(3):
        out = head_ref.at[k] if k < 2 else tail_ref.at[0]
        out[...] = near_ref[0, k] + decode(got_ref.at[0, k])
        encode(near_ref[1, k] + decode(got_ref.at[1, k]), send_ref.at[k])
    ahead_ref[...] = send_ref[:2]


def swap_slabs(slabs):
    lane = lax.broadcasted_iota(jnp.int32, slabs[0].shape, 1)
    width = slabs[0].shape[1]
    slabs = list(slabs)
    for step in (1, 2, 4, 8):
        odd = (lane & step) != 0
        for i in range(len(slabs)):
            if i & step:
                continue
            first, second = slabs[i], slabs[i + step]
            slabs[i] = jnp.where(odd, pltpu.roll(second, step, 1), first)
            slabs[i + step] = jnp.where(odd, second, pltpu.roll(first, width - step, 1))
    return slabs


def swap_rows(slab):
    width = slab.shape[1]
    top, low = slab[:8], slab[8:]
    lane = lax.broadcasted_iota(jnp.int32, top.shape, 1)
    row = lax.broadcasted_iota(jnp.int32, top.shape, 0)
    odd = (lane & 8) != 0
    top, low = (
        jnp.where(odd, pltpu.roll(low, 8, 1), top),
        jnp.where(odd, low, pltpu.roll(top, width - 8, 1)),
    )
    halves = []
    for half in (top, low):
        for step in (1, 2, 4):
            odd_lane, odd_row = (lane & step) != 0, (row & step) != 0
            up = pltpu.roll(pltpu.roll(half, 8 - step, 0), step, 1)
            down = pltpu.roll(pltpu.roll(half, step, 0), width - step, 1)
            other = jnp.where(odd_lane, up, down)
            half = jnp.where(odd_lane == odd_row, half, other)
        halves.append(half)
    return jnp.concatenate(halves, axis=0)


def denoise_kernel(
    offset_ref, p0, p1, p2, p3, up_hbm, down_hbm, near_ref, far_ref, up_ref, down_ref, sems
):
    loads = []
    for k in range(3):
        up = pltpu.make_async_copy(up_hbm.at[k], up_ref.at[k], sems.at[k])
        down = pltpu.make_async_copy(down_hbm.at[k], down_ref.at[k], sems.at[3 + k])
        up.start()
        down.start()
        loads.append((up, down))
    side = PATCH
    size = side * side
    row = lax.broadcasted_iota(jnp.int32, (size, size), 0)
    col = lax.broadcasted_iota(jnp.int32, (size, size), 1)
    turned = (row % side) * side + row // side
    exchange = jnp.where(col == turned, 1.0, 0.0).astype(jnp.bfloat16)
    lane = lax.broadcasted_iota(jnp.int32, (size // 2, WINDOW), 1)
    left = lane < WINDOW // 2
    wide = lax.broadcasted_iota(jnp.int32, (size, WINDOW), 1)

    def joined(a, b):
        a = a.reshape(size // 2, WINDOW).astype(jnp.float32)
        b = b.reshape(size // 2, WINDOW).astype(jnp.float32)
        early = jnp.where(left, a, pltpu.roll(b, WINDOW // 2, 1))
        late = jnp.where(left, pltpu.roll(a, WINDOW // 2, 1), b)
        return jnp.concatenate([early, late], axis=0)

    def slabs_of(half):
        return [half[i * side : (i + 1) * side] for i in range(side)]

    def arrange(which, half):
        if which == 0:
            return jnp.concatenate(swap_slabs(slabs_of(half)), axis=0)
        if which == 2:
            return jnp.concatenate([swap_rows(slab) for slab in slabs_of(half)], axis=0)
        return half

    for k in range(3):
        halves = [joined(p0[k], p1[k]), joined(p2[k], p3[k])]
        if k != 1:
            o = offset_ref[k]
            a, b = [pltpu.roll(half, WINDOW - o, 1) for half in halves]
            inside = wide < WINDOW - o
            halves = [jnp.where(inside, a, b), jnp.where(inside, b, a)]
        halves = [arrange(k, half) for half in halves]
        patches = jnp.concatenate([half.T for half in halves], axis=0).astype(jnp.bfloat16)
        for load in loads[k]:
            load.wait()
        down = down_ref[k]
        if k == 0:
            patches = jnp.dot(
                patches, exchange, preferred_element_type=jnp.float32
            ).astype(jnp.bfloat16)
            down = jnp.dot(down, exchange, preferred_element_type=jnp.float32).astype(jnp.bfloat16)
        hidden = jnp.dot(patches, up_ref[k], preferred_element_type=jnp.float32)
        hidden = jnp.maximum(hidden, 0.0).astype(jnp.bfloat16)
        result = jnp.dot(hidden, down, preferred_element_type=jnp.float32)
        halves = [arrange(k, result[:WINDOW].T), arrange(k, result[WINDOW:].T)]
        if k != 1:
            a, b = [pltpu.roll(half, o, 1) for half in halves]
            inside = wide >= o
            halves = [jnp.where(inside, a, b), jnp.where(inside, b, a)]
        for half, near in ((halves[0], True), (halves[1], False)):
            early, late = half[: size // 2], half[size // 2 :]
            blocks = (
                jnp.where(left, early, pltpu.roll(late, WINDOW // 2, 1)),
                jnp.where(left, pltpu.roll(early, WINDOW // 2, 1), late),
            )
            for j in range(2):
                block = blocks[j].reshape(near_ref.shape[2:])
                if near:
                    near_ref[j, k] = block
                else:
                    encode(block, far_ref.at[j, k])


def spread_kernel(factor, u_ref, rel_ref, w_ref, win_ref, fit_ref, copy_ref):
    angles, planes, _ = win_ref.shape

    def body(a, total):
        band = one_hot(rel_ref[pl.ds(a, 1), :])
        at_low = win_ref[a]
        above = pltpu.roll(at_low, WINDOW - 1, 1)
        terms = jnp.concatenate(split_two(at_low) + split_two(above), axis=0)
        picked = jnp.dot(terms, band, preferred_element_type=jnp.float32)
        near = picked[:planes] + picked[planes : 2 * planes]
        far = picked[2 * planes : 3 * planes] + picked[3 * planes :]
        w = w_ref[pl.ds(a, 1), :]
        return total + (far + w * (near - far))

    total = lax.fori_loop(0, angles, body, jnp.zeros(u_ref.shape, jnp.float32), unroll=16)
    fit = u_ref[...] - factor * total
    rows, cols = fit_ref.shape[2:]
    for x in range(rows):
        fit_ref[0, :, x, :] = fit[:, x * cols : (x + 1) * cols]
    copy_ref[...] = fit_ref[...]


def join_kernel(
    offset_ref, weight_ref, state_ref, fit_ref, head_ref, tail_ref, beside_ref, prev_ref, side_ref,
    next_ref,
):
    planes, _, cols = fit_ref.shape[1:]
    raw = [jnp.full((1, cols), weight_ref[i], jnp.float32) for i in range(4)]
    whole = raw[0] + raw[1] + raw[2] + raw[3]
    share = [value / whole for value in raw]
    row = lax.broadcasted_iota(jnp.int32, tail_ref.shape[1:], 1)
    nets = []
    for k in range(3):
        if k == 2:
            net = tail_ref[0] + decode(beside_ref.at[k])
        else:
            o = offset_ref[k]
            net = head_ref[k] + decode(beside_ref.at[k])
            before = prev_ref[k] + decode(side_ref.at[k])
            net = jnp.where(row >= o, pltpu.roll(net, o, 1), pltpu.roll(before, o, 1))
        nets.append((net[:, :, :cols], pltpu.roll(net, WINDOW - cols, 2)[:, :, :cols]))
    count = planes // 2
    for part in range(2):
        span = slice(part * count, (part + 1) * count)
        held = state_ref[0, 0, span]
        answer = fit_ref[0, span]
        joined = share[0] * (2.0 * answer - held)
        for k in range(3):
            joined = joined + share[k + 1] * (state_ref[k + 1, 0, span] - 2.0 * nets[k][part])
        next_ref[0, 0, span] = held + joined - answer
        for k in range(3):
            next_ref[k + 1, 0, span] = joined + nets[k][part]


VMEM = pl.BlockSpec(memory_space=pltpu.VMEM)
PARAMS = pltpu.CompilerParams(vmem_limit_bytes=20 * 1024 * 1024)
HBM = pl.BlockSpec(memory_space=pltpu.HBM)
SMEM = pl.BlockSpec(memory_space=pltpu.SMEM)


def cost(micros):
    return pl.CostEstimate(flops=micros * 10**9, bytes_accessed=micros * 3 * 10**6, transcendentals=0)


def hop(value, axis, step):
    count = lax.axis_size(axis)
    return lax.ppermute(value, axis, [(i, (i + step) % count) for i in range(count)])


def step(
    agent_state, measured, bin_index, bin_frac, patch_offsets, agent_weights, up_weight, down_weight
):
    planes, row_count, col_count = agent_state.shape[2:]
    tile_count = lax.axis_size("tile")
    agent_count = lax.axis_size("agent")
    angles = bin_index.shape[0]
    pixels = row_count * col_count
    factor = 1.0 / math.sqrt(angles * (row_count * tile_count + col_count * agent_count))
    both = ("tile", "agent")
    f32 = jnp.float32

    shape = (planes // 2, row_count, 2 * col_count)
    coded = (planes // 2 * row_count + 8, 2 * col_count)
    head, tail, volume, bins, nums = pl.pallas_call(
        pack_kernel,
        out_shape=[
            jax.ShapeDtypeStruct((2,) + shape, jnp.bfloat16),
            jax.ShapeDtypeStruct((1,) + shape, jnp.bfloat16),
            jax.ShapeDtypeStruct(agent_state.shape[2:], f32),
            jax.ShapeDtypeStruct(bin_index.shape, jnp.int32),
            jax.ShapeDtypeStruct(bin_frac.shape, jnp.int32),
        ],
        in_specs=[HBM] * 3,
        out_specs=[VMEM] * 5,
        scratch_shapes=[
            pltpu.VMEM((3,) + agent_state.shape[2:], f32),
            pltpu.SemaphoreType.DMA((4,)),
        ],
        compiler_params=pltpu.CompilerParams(vmem_limit_bytes=56000000),
        cost_estimate=cost(2),
        name="pack",
    )(agent_state, bin_index, bin_frac)
    following = hop(head, "tile", -1)

    group = (lax.axis_index("tile") * agent_count // planes).astype(jnp.int32)
    pieces, flat, rel, near = pl.pallas_call(
        project_kernel,
        out_shape=[
            jax.ShapeDtypeStruct((2 * angles * planes, WINDOW), f32),
            jax.ShapeDtypeStruct((planes, pixels), f32),
            jax.ShapeDtypeStruct((angles, pixels), jnp.int32),
            jax.ShapeDtypeStruct((angles, pixels), f32),
        ],
        in_specs=[SMEM] + [VMEM] * 4,
        out_specs=[VMEM] * 4,
        scratch_shapes=[pltpu.VMEM((angles, WINDOW), f32)],
        compiler_params=PARAMS,
        cost_estimate=cost(5),
        name="project",
    )(group.reshape(1), volume, bins, nums, measured)

    region = pl.pallas_call(
        shift_kernel,
        out_shape=jax.ShapeDtypeStruct((3,) + shape, jnp.bfloat16),
        in_specs=[SMEM, VMEM, VMEM, VMEM],
        out_specs=VMEM,
        compiler_params=PARAMS,
        cost_estimate=cost(1),
        name="shift",
    )(patch_offsets, head, tail, following)
    others = []
    for step in range(1, agent_count):
        others.append(hop(region, "agent", -step))

    count = angles * planes
    got = lax.all_to_all(pieces.reshape(count, 2, WINDOW), both, 0, 0, tiled=True)
    cut = pl.pallas_call(
        functools.partial(combine_kernel, factor, measured.shape[2]),
        out_shape=jax.ShapeDtypeStruct((angles * planes, WINDOW), f32),
        in_specs=[VMEM],
        out_specs=VMEM,
        compiler_params=PARAMS,
        cost_estimate=cost(2),
        name="combine",
    )(got.reshape(2 * count, WINDOW))

    back = lax.all_to_all(cut, both, 0, 0, tiled=True)
    own, far = pl.pallas_call(
        denoise_kernel,
        out_shape=[
            jax.ShapeDtypeStruct((2, 3) + shape, f32),
            jax.ShapeDtypeStruct((2, 3) + coded, WIRE),
        ],
        in_specs=[SMEM] + [VMEM] * 4 + [HBM] * 2,
        out_specs=[VMEM] * 2,
        scratch_shapes=[
            pltpu.VMEM(up_weight.shape, up_weight.dtype),
            pltpu.VMEM(down_weight.shape, down_weight.dtype),
            pltpu.SemaphoreType.DMA((6,)),
        ],
        compiler_params=pltpu.CompilerParams(vmem_limit_bytes=54500000),
        cost_estimate=cost(6),
        name="denoise",
    )(patch_offsets, region, *others, up_weight, down_weight)
    opposite = hop(far, "agent", 2)
    head, tail, passed, ahead = pl.pallas_call(
        halve_kernel,
        out_shape=[
            jax.ShapeDtypeStruct((2,) + shape, f32),
            jax.ShapeDtypeStruct((1,) + shape, f32),
            jax.ShapeDtypeStruct((3,) + coded, WIRE),
            jax.ShapeDtypeStruct((2,) + coded, WIRE),
        ],
        in_specs=[VMEM] * 2,
        out_specs=[VMEM] * 4,
        compiler_params=PARAMS,
        cost_estimate=cost(1),
        name="halve",
    )(own, opposite)
    beside = hop(passed, "agent", 1)
    pairs = [
        (t * agent_count + g, (t + 1) % tile_count * agent_count + (g + 1) % agent_count)
        for t in range(tile_count)
        for g in range(agent_count)
    ]
    side = lax.ppermute(ahead, both, pairs)
    previous = hop(head, "tile", 1)

    fit, held = pl.pallas_call(
        functools.partial(spread_kernel, factor),
        out_shape=[jax.ShapeDtypeStruct(agent_state.shape[1:], f32)] * 2,
        in_specs=[VMEM] * 4,
        out_specs=[VMEM] * 2,
        compiler_params=PARAMS,
        cost_estimate=cost(4),
        name="spread",
    )(flat, rel, near, back.reshape(angles, planes, WINDOW))
    state_next = pl.pallas_call(
        join_kernel,
        out_shape=jax.ShapeDtypeStruct(agent_state.shape, f32),
        in_specs=[SMEM, SMEM] + [VMEM] * 7,
        out_specs=VMEM,
        compiler_params=PARAMS,
        cost_estimate=cost(2),
        name="join",
    )(patch_offsets, agent_weights, agent_state, held, head, tail, beside, previous, side)
    return (state_next, fit)


def solution(mesh):
    placed = (
        P(None, None, None, "tile", "agent"),
        P(None, None, ("tile", "agent")),
        P(None, "tile", "agent"),
        P(None, "tile", "agent"),
        P(),
        P(),
        P(None, None, "agent"),
        P(None, "agent", None),
    )
    return jax.shard_map(
        step,
        mesh=mesh,
        in_specs=placed,
        out_specs=(P(None, None, None, "tile", "agent"), P(None, None, "tile", "agent")),
        check_vma=False,
    )
```
